32 devices in a mesh: groups: 2 (over y), rows: 4 (over z), cols: 4 (over x, core).
Axes of the slice: x: 2, y: 2, z: 4, core: 2. Of those that a mesh axis runs over, the one named last changes fastest.
Arguments:
- tokens: bfloat16 [112, 112, 256], P(('groups', 'rows'), 'cols'), parts along dimension 0, may hold values from -6 to 6
- cotangent: bfloat16 [56, 56, 512], P(('groups', 'rows'), 'cols'), parts along dimension 0, may hold values from -6 to 6
- shift_offsets: int32 [4], replicated, may hold values from 1 to 6
- norm2_gain: float32 [256], replicated, may hold values from 0.1 to 1.9
- qkv2: bfloat16 [256, 768], replicated, may hold values from -0.375 to 0.375
- proj2: bfloat16 [256, 256], replicated, may hold values from -0.375 to 0.375
- merge_gain: float32 [1024], replicated, may hold values from 0.1 to 1.9
- merge_weight: bfloat16 [1024, 512], replicated, may hold values from -0.1875 to 0.1875
- norm3_gain: float32 [512], replicated, may hold values from 0.1 to 1.9
- qkv3: bfloat16 [512, 1536], replicated, may hold values from -0.25 to 0.25
- proj3: bfloat16 [512, 512], replicated, may hold values from -0.25 to 0.25
Outputs:
- merged_out: bfloat16 [56, 56, 512], P(('groups', 'rows'), 'cols'), parts along dimension 0
- tokens_grad: bfloat16 [112, 112, 256], P(('groups', 'rows'), 'cols'), parts along dimension 0
- gain_grads: float32 [3584], P('groups'), parts along dimension 0
- qkv2_grad: bfloat16 [393216], P(('groups', 'rows', 'cols')), parts along dimension 0
- proj2_grad: bfloat16 [131072], P(('groups', 'rows', 'cols')), parts along dimension 0
- merge_grad: bfloat16 [1048576], P(('groups', 'rows', 'cols')), parts along dimension 0
- qkv3_grad: bfloat16 [1572864], P(('groups', 'rows', 'cols')), parts along dimension 0
- proj3_grad: bfloat16 [524288], P(('groups', 'rows', 'cols')), parts along dimension 0
The draws below stay inside these ranges and needn't reach their ends.
There are 2 independent parts, one for each index of `groups`. The reference program is written for one: setup_inputs(seed, part) draws one part's arguments, and reference() takes and returns one part's arrays. A program takes and returns all parts, laid end to end along the dimension named above; an argument that names none is the same for every part. Nothing has to cross between parts.
All inputs are finite; a program needn't handle non-finite values.
Results may differ from the reference program's by a relative error of at most 0.033.
Values may be sent and summed in bfloat16 or wider, within the bound.
A program may use at most 128 MiB of HBM per device.

```python
import jax
import jax.numpy as jnp
from jax import lax

C2 = 256
C3 = 512
HEADS2 = 8
HEADS3 = 16
WIN = 7
H2 = 56
W2 = 112


def plant(array, key, smallest, top_value):
    extent = array.shape
    place = [jax.random.randint(jax.random.fold_in(key, axis), (), 0, extent[axis]) for axis in range(len(extent))]
    array = array.at[tuple(place)].set(smallest)
    longest = extent.index(max(extent))
    place[longest] = (place[longest] + 1) % extent[longest]
    return array.at[tuple(place)].set(top_value)


def shard_levels(own_key, shape, split, least, top_value):
    level = 1.0
    for dim, parts in split:
        heights = jax.random.uniform(jax.random.fold_in(jax.random.fold_in(own_key, 6), dim), (parts,), jnp.float32, least / len(split), top_value / len(split))
        level = level * jnp.repeat(jnp.exp(heights), shape[dim] // parts).reshape((-1,) + (1,) * (len(shape) - 1 - dim))
    return level


def noise(rng, extent, scale, bound, pieces=(), kind=jnp.bfloat16):
    result = jax.random.normal(rng, extent, jnp.float32) * scale
    if len(pieces) > 0:
        result = shard_levels(rng, extent, pieces, -0.22, 0.18) * result
    return jnp.clip(result, min=-bound, max=bound).astype(kind)


def setup_inputs(seed: int = 0, part: int = 0) -> dict:
    splits = jax.random.split(jax.random.key(seed), 12)
    part_splits = jax.random.split(jax.random.fold_in(splits[11], part), 12)
    return {
        "tokens": noise(part_splits[0], (H2, W2, C2), 1.0, 6.0, ((0, 4), (1, 4))),
        "cotangent": noise(part_splits[1], (H2 // 2, W2 // 2, C3), 1.0, 6.0, ((0, 4), (1, 4))),
        "shift_offsets": plant(jax.random.randint(splits[2], (4,), 1, WIN), jax.random.fold_in(splits[2], 1), 1, WIN - 1).astype(jnp.int32),
        "norm2_gain": jnp.clip(1.0 + 0.18 * jax.random.normal(splits[3], (C2,), jnp.float32), 0.1, 1.9),
        "qkv2": noise(splits[4], (C2, 3 * C2), C2 ** -0.5, 0.375),
        "proj2": noise(splits[5], (C2, C2), C2 ** -0.5, 0.375),
        "merge_gain": jnp.clip(1.0 + 0.18 * jax.random.normal(splits[6], (4 * C2,), jnp.float32), 0.1, 1.9),
        "merge_weight": noise(splits[7], (4 * C2, C3), (4 * C2) ** -0.5, 0.1875),
        "norm3_gain": jnp.clip(1.0 + 0.18 * jax.random.normal(splits[8], (C3,), jnp.float32), 0.1, 1.9),
        "qkv3": noise(splits[9], (C3, 3 * C3), C3 ** -0.5, 0.25),
        "proj3": noise(splits[10], (C3, C3), C3 ** -0.5, 0.25),
    }


EPSILON = 1e-05
MASKED = -100.0

def normalize(inputs, gain):
    widened = inputs.astype(jnp.float32)
    centred = widened - lax.optimization_barrier(jnp.mean(widened, axis=-1, keepdims=True))
    spread = lax.optimization_barrier(jnp.mean(centred * centred, axis=-1, keepdims=True))
    return (centred * lax.rsqrt(spread + EPSILON) * gain).astype(jnp.bfloat16)

def attend(packed, heads, region):
    count, window_area, triple = packed.shape
    width = triple // 3
    head_size = width // heads
    queries = packed[:, :, :width].astype(jnp.float32).reshape(count, window_area, heads, head_size)
    key_part = packed[:, :, width:2 * width].astype(jnp.float32).reshape(count, window_area, heads, head_size)
    values = packed[:, :, 2 * width:].astype(jnp.float32).reshape(count, window_area, heads, head_size)
    scores = jnp.einsum('nphd,nqhd->nhpq', queries, key_part) * head_size ** (-0.5)
    scores = scores + region[:, None, :, :]
    raised = jnp.exp(scores)
    weights = (raised / lax.optimization_barrier(jnp.sum(raised, axis=-1, keepdims=True))).astype(jnp.bfloat16)
    mixed = jnp.einsum('nhpq,nqhd->nphd', weights.astype(jnp.float32), values)
    return mixed.reshape(count, window_area, width).astype(jnp.bfloat16)

def to_windows(values, window):
    height, breadth, width = values.shape
    shaped = values.reshape(height // window, window, breadth // window, window, width)
    return shaped.transpose(0, 2, 1, 3, 4).reshape(-1, window * window, width)

def from_windows(windows, height, breadth, window):
    width = windows.shape[-1]
    shaped = windows.reshape(height // window, breadth // window, window, window, width)
    return shaped.transpose(0, 2, 1, 3, 4).reshape(height, breadth, width)

def pair_join(values):
    height, breadth, width = values.shape
    shaped = values.reshape(height // 2, 2, breadth // 2, 2, width)
    return shaped.transpose(0, 2, 3, 1, 4).reshape(height // 2, breadth // 2, 4 * width)

def cyclic(values, start, axis):
    doubled = jnp.concatenate([values, values], axis=axis)
    return lax.dynamic_slice_in_dim(doubled, start.astype(jnp.int32), values.shape[axis], axis)

def region_bias(row_coords, col_coords, height, breadth, shift_rows, shift_cols):
    row_label = jnp.where(row_coords < height - WIN, 0, jnp.where(row_coords < height - shift_rows, 1, 2))
    col_label = jnp.where(col_coords < breadth - WIN, 0, jnp.where(col_coords < breadth - shift_cols, 1, 2))
    labels = (row_label[:, None] * 3 + col_label[None, :]).astype(jnp.int32)
    windowed = to_windows(labels[:, :, None], WIN)[:, :, 0]
    return jnp.where(windowed[:, :, None] == windowed[:, None, :], 0.0, MASKED).astype(jnp.float32)

def shifted_block(inputs, normed, shift_rows, shift_cols, qkv, proj, heads):
    height, breadth, width = inputs.shape
    rolled = to_windows(cyclic(cyclic(normed, shift_rows, 0), shift_cols, 1), WIN)
    bias = region_bias(jnp.arange(height, dtype=jnp.int32), jnp.arange(breadth, dtype=jnp.int32), height, breadth, shift_rows, shift_cols)
    packed = jnp.dot(rolled.reshape(-1, width), qkv, preferred_element_type=jnp.float32)
    packed = packed.astype(jnp.bfloat16).reshape(rolled.shape[0], WIN * WIN, 3 * width)
    mixed = attend(packed, heads, bias)
    projected = jnp.dot(mixed.reshape(-1, width), proj, preferred_element_type=jnp.float32).astype(jnp.bfloat16)
    grid = from_windows(projected.reshape(-1, WIN * WIN, width), height, breadth, WIN)
    restored = cyclic(cyclic(grid, height - shift_rows, 0), breadth - shift_cols, 1)
    return (inputs.astype(jnp.float32) + restored.astype(jnp.float32)).astype(jnp.bfloat16)

def forward(tokens, norm2_gain, qkv2, proj2, merge_gain, merge_weight, norm3_gain, qkv3, proj3, shift_offsets):
    height, breadth, narrow = tokens.shape
    wide_width = qkv3.shape[0]
    normed = normalize(tokens, norm2_gain)
    section_two = shifted_block(tokens, normed, shift_offsets[0], shift_offsets[1], qkv2, proj2, HEADS2)
    merged_norm = normalize(pair_join(section_two), merge_gain)
    merged = jnp.dot(merged_norm.reshape(-1, 4 * narrow), merge_weight, preferred_element_type=jnp.float32)
    merged = merged.astype(jnp.bfloat16).reshape(height // 2, breadth // 2, wide_width)
    normed_three = normalize(merged, norm3_gain)
    return shifted_block(merged, normed_three, shift_offsets[2], shift_offsets[3], qkv3, proj3, HEADS3)

def reference(tokens, cotangent, shift_offsets, norm2_gain, qkv2, proj2, merge_gain, merge_weight, norm3_gain, qkv3, proj3):

    def run(tok, gain_two, weight_qkv2, weight_proj2, gain_merge, weight_merge, gain_three, weight_qkv3, weight_proj3):
        return forward(tok, gain_two, weight_qkv2, weight_proj2, gain_merge, weight_merge, gain_three, weight_qkv3, weight_proj3, shift_offsets)
    outcome, pullback = jax.vjp(run, tokens, norm2_gain, qkv2, proj2, merge_gain, merge_weight, norm3_gain, qkv3, proj3)
    grads = pullback(cotangent)
    gains = jnp.concatenate([grads[1], grads[4], grads[6]])
    return (outcome, grads[0], gains, grads[2].reshape(-1), grads[3].reshape(-1), grads[5].reshape(-1), grads[7].reshape(-1), grads[8].reshape(-1))
```

```python
import functools

import jax
import jax.numpy as jnp
import numpy as np
from jax import lax
from jax.experimental import pallas as pl
from jax.experimental.pallas import tpu as pltpu
from jax.sharding import PartitionSpec as P

HEAD = 32
WIN = 7
MARGIN = WIN - 1
SLOT = 64
PM = 16
LANES = 128
EPSILON = 1e-05
MASKED = -100.0
F32 = jnp.float32
BF16 = jnp.bfloat16


def pitch_of(count):
    return -(-count // 16) * 16


def window_tokens(rows, cols):
    h, w, ok = [], [], []
    for wr in range(rows // WIN):
        for wc in range(cols // WIN):
            for t in range(SLOT):
                good = t < WIN * WIN
                h.append(wr * WIN + t // WIN if good else 0)
                w.append(wc * WIN + t % WIN if good else 0)
                ok.append(good)
    return np.array(h, np.int32), np.array(w, np.int32), np.array(ok)


def grid_tokens(rows, cols, pitch):
    h = np.repeat(np.arange(rows, dtype=np.int32), pitch)
    w = np.tile(np.arange(pitch, dtype=np.int32), rows)
    ok = w < cols
    return h, np.where(ok, w, 0).astype(np.int32), ok


def quad_tokens(rows, cols):
    a, b, ok = grid_tokens(rows // 2, cols // 2, pitch_of(cols // 2))
    h = np.concatenate([2 * a + (k & 1) for k in range(4)])
    w = np.concatenate([2 * b + (k >> 1) for k in range(4)])
    return h, w, np.tile(ok, 4)


def win_index(h, w, cols):
    return ((h // WIN) * (cols // WIN) + w // WIN) * SLOT + (h % WIN) * WIN + w % WIN


def quad_index(h, w, rows, cols):
    pitch = pitch_of(cols // 2)
    return ((h % 2) + 2 * (w % 2)) * ((rows // 2) * pitch) + (h // 2) * pitch + w // 2


def ahead_index(h, w, ok, shift_rows, shift_cols, rows, cols, inner, base):
    pitch = pitch_of(cols)
    h2, w2 = h + shift_rows, w + shift_cols
    local = inner(jnp.minimum(h2, rows - 1), jnp.minimum(w2, cols - 1))
    below = base + (h2 - rows) * pitch + w2
    side = base + MARGIN * pitch + h2 * PM + (w2 - cols)
    idx = jnp.where(w2 >= cols, side, jnp.where(h2 >= rows, below, local))
    return jnp.where(ok, idx, -1).astype(jnp.int32).reshape(-1, 1)


def behind_index(h, w, ok, shift_rows, shift_cols, rows, cols, base):
    pitch = pitch_of(cols)
    h2, w2 = h - shift_rows, w - shift_cols
    local = win_index(jnp.maximum(h2, 0), jnp.maximum(w2, 0), cols)
    above = base + (h2 + MARGIN) * pitch + w2
    row = jnp.where(h2 >= 0, h2, rows + h2 + MARGIN)
    side = base + MARGIN * pitch + row * PM + (w2 + MARGIN)
    idx = jnp.where(w2 < 0, side, jnp.where(h2 < 0, above, local))
    return jnp.where(ok, idx, -1).astype(jnp.int32).reshape(-1, 1)


def piece_index(rows, cols, inner, first):
    top = 0 if first else rows - MARGIN
    left = 0 if first else cols - MARGIN
    parts = []
    for count, wide, pitch, h0, w0 in (
        (MARGIN, cols, pitch_of(cols), top, 0),
        (rows, MARGIN, PM, 0, left),
        (MARGIN, MARGIN, PM, top, left),
    ):
        h, w, ok = grid_tokens(count, wide, pitch)
        parts.append(np.where(ok, inner(h + h0, w + w0), -1))
    return np.concatenate(parts).astype(np.int32).reshape(-1, 1)


def piece_sizes(rows, cols):
    return MARGIN * pitch_of(cols), rows * PM, MARGIN * PM


def window_labels(rows, cols, axis_row, axis_col, shift_rows, shift_cols):
    h, w, ok = window_tokens(rows, cols)
    height = rows * lax.axis_size("rows")
    breadth = cols * lax.axis_size("cols")
    gh = axis_row * rows + h
    gw = axis_col * cols + w
    lh = jnp.where(gh < height - WIN, 0, jnp.where(gh < height - shift_rows, 1, 2))
    lw = jnp.where(gw < breadth - WIN, 0, jnp.where(gw < breadth - shift_cols, 1, 2))
    flat = jnp.where(ok, lh * 3 + lw, -1).astype(jnp.int32)
    return flat.reshape(-1, 1), flat.reshape(-1, SLOT)


def dot(a, b):
    return jnp.dot(a, b, preferred_element_type=F32)


def dot_nt(a, b):
    return lax.dot_general(a, b, (((1,), (1,)), ((), ())), preferred_element_type=F32)


def dot_tn(a, b):
    return lax.dot_general(a, b, (((0,), (0,)), ((), ())), preferred_element_type=F32)


def select(idx, source):
    count = source.shape[0]
    lane = lax.broadcasted_iota(jnp.int32, (idx.shape[0], count), 1)
    hot = jnp.where(idx == lane, 1.0, 0.0).astype(BF16)
    return dot(hot, source).astype(BF16)


def norm_parts(x):
    centred = x - jnp.mean(x, axis=-1, keepdims=True)
    inverse = lax.rsqrt(jnp.mean(centred * centred, axis=-1, keepdims=True) + EPSILON)
    return centred * inverse, inverse


def norm_back(hat, inverse, gain, dy):
    grad_gain = jnp.sum(dy * hat, axis=0, keepdims=True)
    t = dy * gain
    dx = inverse * (
        t
        - jnp.mean(t, axis=-1, keepdims=True)
        - hat * jnp.mean(t * hat, axis=-1, keepdims=True)
    )
    return dx.astype(BF16), grad_gain


PACK = LANES // HEAD


def head_masks():
    lane = lax.broadcasted_iota(jnp.int32, (1, LANES), 1) // HEAD
    return [jnp.where(lane == h, 1.0, 0.0).astype(BF16) for h in range(PACK)]


def stack_heads(x, masks):
    return jnp.concatenate([x * m for m in masks], axis=0)


def pick_heads(o):
    lane = lax.broadcasted_iota(jnp.int32, (SLOT, LANES), 1) // HEAD
    out = o[:SLOT]
    for h in range(1, PACK):
        out = jnp.where(lane == h, o[h * SLOT : (h + 1) * SLOT], out)
    return out


def window_bias(lc_ref, lr_ref, w):
    lc = lc_ref[w * SLOT : (w + 1) * SLOT, :]
    lr = lr_ref[w : w + 1, :]
    bias = jnp.where((lc == lr) | (lc < 0), 0.0, MASKED)
    bias = jnp.where(lr < 0, -1e30, bias)
    return jnp.concatenate([bias] * PACK, axis=0)


def soft(qs, k, bias):
    raised = jnp.exp(dot_nt(qs, k) * HEAD ** (-0.5) + bias)
    return raised * (1.0 / jnp.sum(raised, axis=-1, keepdims=True))


def unit_back(qs, k, v, weights, wb, dm, masks):
    dms = stack_heads(dm, masks)
    dw = dot_nt(dms, v).astype(BF16).astype(F32)
    ds = weights * (dw - jnp.sum(dw * weights, axis=-1, keepdims=True))
    ds = (ds * HEAD ** (-0.5)).astype(BF16)
    dq = pick_heads(dot(ds, k))
    dk = dot_tn(ds, qs)
    dv = dot_tn(wb, dms)
    return dq.astype(BF16), dk.astype(BF16), dv.astype(BF16)


def fill_tile(scratch, tile, pitch):
    count, wide, _ = tile.shape
    for r in range(count):
        scratch[r * pitch : r * pitch + wide, :] = tile[r]


def fill_ext(scratch, tile, below, side, corner):
    rows, cols, _ = tile.shape
    pitch = pitch_of(cols)
    scratch[...] = jnp.zeros_like(scratch)
    fill_tile(scratch, tile, pitch)
    base = rows * pitch
    for r in range(MARGIN):
        scratch[base + r * pitch : base + r * pitch + cols, :] = below[r]
    base += MARGIN * pitch
    for r in range(rows):
        scratch[base + r * PM : base + r * PM + MARGIN, :] = side[r]
    for r in range(MARGIN):
        scratch[base + (rows + r) * PM : base + (rows + r) * PM + MARGIN, :] = corner[r]


def put_pieces(idx, source, row_ref, col_ref, corner_ref):
    got = select(idx[...], source)
    a, b = row_ref.shape[0], col_ref.shape[0]
    row_ref[...] = got[:a]
    col_ref[...] = got[a : a + b]
    corner_ref[...] = got[a + b :]


def kernel_one(
    tok, below, side, corner, idx_a, idx_q, idx_p, lc, lr, gain, qkv, proj,
    rolled, packed, mixed, win, quad, p_row, p_col, p_cor, ext,
):
    width = proj.shape[0]
    fill_ext(ext, tok, below, side, corner)
    pitch = pitch_of(tok.shape[1])
    quad[...] = select(idx_q[...], ext[: tok.shape[0] * pitch, :])
    hat, _ = norm_parts(select(idx_a[...], ext[...]).astype(F32))
    normed = (hat * gain[...]).astype(BF16)
    rolled[...] = normed
    packed[...] = dot(normed, qkv[...]).astype(BF16)
    masks = head_masks()
    for w in range(lr.shape[0]):
        bias = window_bias(lc, lr, w)
        at = slice(w * SLOT, (w + 1) * SLOT)
        for g in range(width // LANES):
            lanes = [slice(t * width + g * LANES, t * width + (g + 1) * LANES) for t in range(3)]
            qs = stack_heads(packed[at, lanes[0]], masks)
            wb = soft(qs, packed[at, lanes[1]], bias).astype(BF16)
            mixed[at, lanes[0]] = pick_heads(dot(wb, packed[at, lanes[2]])).astype(BF16)
    out = dot(mixed[...], proj[...]).astype(BF16)
    win[...] = out
    put_pieces(idx_p, out, p_row, p_col, p_cor)


def kernel_two(win, below, side, corner, idx, quad, gain_m, weight, gain_3, section, merged, normed3):
    ext = jnp.concatenate([win[...], below[...], side[...], corner[...]], axis=0)
    restored = select(idx[...], ext)
    total = (quad[...].astype(F32) + restored.astype(F32)).astype(BF16)
    section[...] = total
    t3 = merged.shape[0]
    joined = jnp.concatenate([total[k * t3 : (k + 1) * t3] for k in range(4)], axis=1)
    hat, _ = norm_parts(joined.astype(F32))
    out = dot((hat * gain_m[...]).astype(BF16), weight[...]).astype(BF16)
    merged[...] = out
    hat3, _ = norm_parts(out.astype(F32))
    normed3[...] = (hat3 * gain_3[...]).astype(BF16)


def kernel_three(
    tile, below, side, corner, cot, c_below, c_side, c_corner, idx_a, idx_p, lc, lr, qkv, proj,
    both, p_row, p_col, p_cor, grads, ext, packed, mixed, dpacked,
):
    width = proj.shape[0]
    fill_ext(ext, cot, c_below, c_side, c_corner)
    idx = idx_a[...]
    dproj = select(idx, ext[...])
    rolled = select(
        idx, jnp.concatenate([tile[...], below[...], side[...], corner[...]], axis=0)
    )
    packed[...] = dot(rolled, qkv[...]).astype(BF16)
    dmixed = dot_nt(dproj, proj[...]).astype(BF16)
    masks = head_masks()
    for w in range(lr.shape[0]):
        bias = window_bias(lc, lr, w)
        at = slice(w * SLOT, (w + 1) * SLOT)
        for g in range(width // LANES):
            lanes = [slice(t * width + g * LANES, t * width + (g + 1) * LANES) for t in range(3)]
            qs = stack_heads(packed[at, lanes[0]], masks)
            k, v = packed[at, lanes[1]], packed[at, lanes[2]]
            weights = soft(qs, k, bias)
            wb = weights.astype(BF16)
            mixed[at, lanes[0]] = pick_heads(dot(wb, v)).astype(BF16)
            back = unit_back(qs, k, v, weights, wb, dmixed[at, lanes[0]], masks)
            for t in range(3):
                dpacked[at, lanes[t]] = back[t]
    both[:, :width] = dot(mixed[...], proj[...]).astype(BF16)
    both[:, width:] = dot_nt(dpacked[...], qkv[...]).astype(BF16)
    put_pieces(idx_p, both[...], p_row, p_col, p_cor)
    grads[:, : 3 * width] = dot_tn(rolled, dpacked[...]).astype(BF16)
    grads[:, 3 * width :] = dot_tn(mixed[...], dproj).astype(BF16)


def kernel_four(
    both, below, side, corner, idx, idx_p, cot, merged, section, gain_m, gain_3, weight,
    out, dsec, p_row, p_col, p_cor, grad, g_m, g_3, cots,
):
    width = merged.shape[1]
    rows, cols, _ = cot.shape
    pitch = pitch_of(cols)
    cots[...] = jnp.zeros_like(cots)
    fill_tile(cots, cot, pitch)
    ext = jnp.concatenate([both[...], below[...], side[...], corner[...]], axis=0)
    back = select(idx[...], ext)
    mine = merged[...].astype(F32)
    total = (mine + back[:, :width].astype(F32)).astype(BF16)
    for r in range(rows):
        out[r] = total[r * pitch : r * pitch + cols]
    hat3, inv3 = norm_parts(mine)
    dmerged, grad3 = norm_back(hat3, inv3, gain_3[...], back[:, width:].astype(F32))
    g_3[...] = grad3
    dmerged = cots[...] + dmerged
    t3 = merged.shape[0]
    joined = jnp.concatenate([section[k * t3 : (k + 1) * t3, :] for k in range(4)], axis=1)
    hat, inv = norm_parts(joined.astype(F32))
    normed = (hat * gain_m[...]).astype(BF16)
    djn = dot_nt(dmerged, weight[...]).astype(BF16).astype(F32)
    djoined, gradm = norm_back(hat, inv, gain_m[...], djn)
    g_m[...] = gradm
    narrow = dsec.shape[1]
    ds = jnp.concatenate([djoined[:, k * narrow : (k + 1) * narrow] for k in range(4)], axis=0)
    dsec[...] = ds
    put_pieces(idx_p, ds, p_row, p_col, p_cor)
    grad[...] = dot_tn(normed, dmerged).astype(BF16)


def kernel_five(
    dsec, below, side, corner, idx_a, idx_p, lc, lr, packed, rolled, mixed, qkv, proj,
    drolled, p_row, p_col, p_cor, grads, dpacked,
):
    width = proj.shape[0]
    ext = jnp.concatenate([dsec[...], below[...], side[...], corner[...]], axis=0)
    dproj = select(idx_a[...], ext)
    dmixed = dot_nt(dproj, proj[...]).astype(BF16)
    masks = head_masks()
    for w in range(lr.shape[0]):
        bias = window_bias(lc, lr, w)
        at = slice(w * SLOT, (w + 1) * SLOT)
        for g in range(width // LANES):
            lanes = [slice(t * width + g * LANES, t * width + (g + 1) * LANES) for t in range(3)]
            qs = stack_heads(packed[at, lanes[0]], masks)
            k, v = packed[at, lanes[1]], packed[at, lanes[2]]
            weights = soft(qs, k, bias)
            back = unit_back(
                qs, k, v, weights, weights.astype(BF16), dmixed[at, lanes[0]], masks
            )
            for t in range(3):
                dpacked[at, lanes[t]] = back[t]
    out = dot_nt(dpacked[...], qkv[...]).astype(BF16)
    drolled[...] = out
    put_pieces(idx_p, out, p_row, p_col, p_cor)
    grads[:, : 3 * width] = dot_tn(rolled[...], dpacked[...]).astype(BF16)
    grads[:, 3 * width :] = dot_tn(mixed[...], dproj).astype(BF16)


def kernel_six(win, below, side, corner, idx, idx_n, tok, dsec, gain, out, g_2, toks):
    rows, cols, _ = tok.shape
    pitch = pitch_of(cols)
    toks[...] = jnp.zeros_like(toks)
    fill_tile(toks, tok, pitch)
    ext = jnp.concatenate([win[...], below[...], side[...], corner[...]], axis=0)
    dnormed = select(idx[...], ext).astype(F32)
    hat, inv = norm_parts(toks[...].astype(F32))
    dtok, grad = norm_back(hat, inv, gain[...], dnormed)
    g_2[...] = grad
    total = select(idx_n[...], dsec[...]) + dtok
    for r in range(rows):
        out[r] = total[r * pitch : r * pitch + cols]


def call(kernel, outs, scratch, name, args, cost=12e6):
    return pl.pallas_call(
        kernel,
        out_shape=[jax.ShapeDtypeStruct(s, d) for s, d in outs],
        scratch_shapes=[pltpu.VMEM(s, BF16) for s in scratch],
        cost_estimate=pl.CostEstimate(flops=10**9, bytes_accessed=int(cost), transcendentals=0),
        name=name,
    )(*args)


def passed_along(value, axis, by):
    count = lax.axis_size(axis)
    return lax.ppermute(value, axis, [(i, (i + by) % count) for i in range(count)])


def passed_diagonal(value, by):
    nr, nc = lax.axis_size("rows"), lax.axis_size("cols")
    pairs = [
        (r * nc + c, ((r + by) % nr) * nc + (c + by) % nc) for r in range(nr) for c in range(nc)
    ]
    return lax.ppermute(value, ("rows", "cols"), pairs)


def exchange(pieces, by):
    row, col, corner = pieces
    return (
        passed_along(row, "rows", by),
        passed_along(col, "cols", by),
        passed_diagonal(corner, by),
    )


def add_up(terms):
    total = terms[0].astype(F32)
    for term in terms[1:]:
        total = total + term.astype(F32)
    return total


def scatter_sum(grads):
    nr, nc = lax.axis_size("rows"), lax.axis_size("cols")
    chips = nc // 2
    me = lax.axis_index("cols")
    core, chip, row = me % 2, me // 2, lax.axis_index("rows")
    depth, width = grads.shape
    parts = grads.reshape(nr, chips, 2, depth // (nr * nc), width)
    keep = lax.dynamic_index_in_dim(parts, core, 2, keepdims=False)
    send = lax.dynamic_index_in_dim(parts, 1 - core, 2, keepdims=False)
    got = lax.ppermute(send, "cols", [(i, i ^ 1) for i in range(nc)])
    half = add_up([keep, got]).astype(BF16)
    terms = [lax.dynamic_index_in_dim(half, chip, 1, keepdims=False)]
    for d in range(1, chips):
        send = lax.dynamic_index_in_dim(half, (chip + d) % chips, 1, keepdims=False)
        pairs = [(i, (i + 2 * d) % nc) for i in range(nc)]
        terms.append(lax.ppermute(send, "cols", pairs))
    part = add_up(terms).astype(BF16)
    terms = [lax.dynamic_index_in_dim(part, row, 0, keepdims=False)]
    for d in range(1, nr):
        send = lax.dynamic_index_in_dim(part, (row + d) % nr, 0, keepdims=False)
        terms.append(passed_along(send, "rows", d))
    return add_up(terms).astype(BF16)


def sum_all(value):
    nr, nc = lax.axis_size("rows"), lax.axis_size("cols")
    value = value + lax.ppermute(value, "cols", [(i, i ^ 1) for i in range(nc)])
    total = value
    for d in range(1, nc // 2):
        total = total + lax.ppermute(value, "cols", [(i, (i + 2 * d) % nc) for i in range(nc)])
    value = total
    for d in range(1, nr):
        total = total + passed_along(value, "rows", d)
    return total


def on_device(
    tokens, cotangent, shifts, norm2_gain, qkv2, proj2, merge_gain, merge_weight, norm3_gain,
    qkv3, proj3,
):
    rows, cols, narrow = tokens.shape
    wide = qkv3.shape[0]
    rows3, cols3 = rows // 2, cols // 2
    pitch, pitch3 = pitch_of(cols), pitch_of(cols3)
    base, base3 = rows * pitch, rows3 * pitch3
    r, c = lax.axis_index("rows"), lax.axis_index("cols")
    s0, s1, s2, s3 = shifts[0], shifts[1], shifts[2], shifts[3]

    win2, win3 = window_tokens(rows, cols), window_tokens(rows3, cols3)
    n2, n3 = len(win2[0]), len(win3[0])
    quad = quad_tokens(rows, cols)
    nat = grid_tokens(rows, cols, pitch)
    grid3 = grid_tokens(rows3, cols3, pitch3)
    as_grid = lambda h, w: h * pitch + w
    as_grid3 = lambda h, w: h * pitch3 + w
    as_quad = lambda h, w: quad_index(h, w, rows, cols)
    as_win = lambda h, w: win_index(h, w, cols)
    as_win3 = lambda h, w: win_index(h, w, cols3)
    fixed = lambda t, inner: np.where(t[2], inner(t[0], t[1]), -1).astype(np.int32).reshape(-1, 1)

    idx_a = ahead_index(*win2, s0, s1, rows, cols, as_grid, base)
    idx_h = ahead_index(*win2, s0, s1, rows, cols, as_quad, len(quad[0]))
    idx_d = ahead_index(*win3, s2, s3, rows3, cols3, as_grid3, base3)
    idx_c = behind_index(*quad, s0, s1, rows, cols, n2)
    idx_i = behind_index(*nat, s0, s1, rows, cols, n2)
    idx_f = behind_index(*grid3, s2, s3, rows3, cols3, n3)
    idx_q = fixed(quad, as_grid)
    idx_n = fixed(nat, as_quad)
    idx_b = piece_index(rows, cols, as_win, False)
    idx_e = piece_index(rows3, cols3, as_win3, False)
    idx_g = piece_index(rows, cols, as_quad, True)
    lc2, lr2 = window_labels(rows, cols, r, c, s0, s1)
    lc3, lr3 = window_labels(rows3, cols3, r, c, s2, s3)
    gain2, gainm, gain3 = (g.reshape(1, -1) for g in (norm2_gain, merge_gain, norm3_gain))

    def first(x):
        return x[:MARGIN], x[:, :MARGIN], x[:MARGIN, :MARGIN]

    sizes = piece_sizes(rows, cols)
    sizes3 = piece_sizes(rows3, cols3)
    ext = base + MARGIN * pitch + (rows + MARGIN) * PM
    ext3 = base3 + MARGIN * pitch3 + (rows3 + MARGIN) * PM
    quads = len(quad[0])

    tok_halo = exchange(first(tokens), -1)
    cot_halo = exchange(first(cotangent), -1)

    rolled, packed, mixed, win, tquad, *pieces = call(
        kernel_one,
        [((n2, narrow), BF16), ((n2, 3 * narrow), BF16), ((n2, narrow), BF16),
         ((n2, narrow), BF16), ((quads, narrow), BF16)]
        + [((s, narrow), BF16) for s in sizes],
        [(ext, narrow)],
        "section_two",
        (tokens, *tok_halo, idx_a, idx_q, idx_b, lc2, lr2, gain2, qkv2, proj2),
    )
    halo = exchange(pieces, 1)
    section, merged, normed3 = call(
        kernel_two,
        [((quads, narrow), BF16), ((base3, wide), BF16), ((base3, wide), BF16)],
        [],
        "merge",
        (win, *halo, idx_c, tquad, gainm, merge_weight, gain3),
    )
    if PM == pitch3:
        side3 = normed3
    else:
        side3 = normed3.reshape(rows3, pitch3, wide)[:, :PM].reshape(rows3 * PM, wide)
    corner3 = side3[: MARGIN * PM]
    halo = exchange((normed3[: MARGIN * pitch3], side3, corner3), -1)
    both, p_row, p_col, p_cor, grads3 = call(
        kernel_three,
        [((n3, 2 * wide), BF16)]
        + [((s, 2 * wide), BF16) for s in sizes3]
        + [((wide, 4 * wide), BF16)],
        [(ext3, wide), (n3, 3 * wide), (n3, wide), (n3, 3 * wide)],
        "section_three",
        (normed3, *halo, cotangent, *cot_halo, idx_d, idx_e, lc3, lr3, qkv3, proj3),
    )
    halo = exchange((p_row, p_col, p_cor), 1)
    out, dsec, p_row, p_col, p_cor, grads_m, g_m, g_3 = call(
        kernel_four,
        [(cotangent.shape, BF16), ((quads, narrow), BF16)]
        + [((s, narrow), BF16) for s in sizes]
        + [((4 * narrow, wide), BF16), ((1, 4 * narrow), F32), ((1, wide), F32)],
        [(base3, wide)],
        "merge_back",
        (both, *halo, idx_f, idx_g, cotangent, merged, section, gainm, gain3, merge_weight),
    )
    halo = exchange((p_row, p_col, p_cor), -1)
    drolled, p_row, p_col, p_cor, grads2 = call(
        kernel_five,
        [((n2, narrow), BF16)]
        + [((s, narrow), BF16) for s in sizes]
        + [((narrow, 4 * narrow), BF16)],
        [(n2, 3 * narrow)],
        "section_two_back",
        (dsec, *halo, idx_h, idx_b, lc2, lr2, packed, rolled, mixed, qkv2, proj2),
    )
    halo = exchange((p_row, p_col, p_cor), 1)
    tokens_grad, g_2 = call(
        kernel_six,
        [(tokens.shape, BF16), ((1, narrow), F32)],
        [(base, narrow)],
        "tokens_back",
        (drolled, *halo, idx_i, idx_n, tokens, dsec, gain2),
    )
    sum3, sum_m, sum2 = scatter_sum(grads3), scatter_sum(grads_m), scatter_sum(grads2)
    gains = sum_all(jnp.concatenate([g_2, g_m, g_3], axis=1)).reshape(-1)
    return (
        out,
        tokens_grad,
        gains,
        sum2[:, : 3 * narrow].reshape(-1),
        sum2[:, 3 * narrow :].reshape(-1),
        sum_m.reshape(-1),
        sum3[:, : 3 * wide].reshape(-1),
        sum3[:, 3 * wide :].reshape(-1),
    )


def solution(mesh):
    tile = P(("groups", "rows"), "cols", None)
    spread = P(("groups", "rows", "cols"))
    return jax.shard_map(
        on_device,
        mesh=mesh,
        in_specs=(tile, tile) + (P(),) * 9,
        out_specs=(tile, tile, P("groups")) + (spread,) * 5,
        check_vma=False,
    )
```

```python
import functools

import jax
import jax.numpy as jnp
import numpy as np
from jax import lax
from jax.experimental import pallas as pl
from jax.experimental.pallas import tpu as pltpu
from jax.sharding import PartitionSpec as P

HEAD = 32
WIN = 7
MARGIN = WIN - 1
SLOT = 64
PM = 16
LANES = 128
EPSILON = 1e-05
MASKED = -100.0
F32 = jnp.float32
BF16 = jnp.bfloat16


def pitch_of(count):
    return -(-count // 16) * 16


def window_tokens(rows, cols):
    h, w, ok = [], [], []
    for wr in range(rows // WIN):
        for wc in range(cols // WIN):
            for t in range(SLOT):
                good = t < WIN * WIN
                h.append(wr * WIN + t // WIN if good else 0)
                w.append(wc * WIN + t % WIN if good else 0)
                ok.append(good)
    return np.array(h, np.int32), np.array(w, np.int32), np.array(ok)


def grid_tokens(rows, cols, pitch):
    h = np.repeat(np.arange(rows, dtype=np.int32), pitch)
    w = np.tile(np.arange(pitch, dtype=np.int32), rows)
    ok = w < cols
    return h, np.where(ok, w, 0).astype(np.int32), ok


def quad_tokens(rows, cols):
    a, b, ok = grid_tokens(rows // 2, cols // 2, pitch_of(cols // 2))
    h = np.concatenate([2 * a + (k & 1) for k in range(4)])
    w = np.concatenate([2 * b + (k >> 1) for k in range(4)])
    return h, w, np.tile(ok, 4)


def win_index(h, w, cols):
    return ((h // WIN) * (cols // WIN) + w // WIN) * SLOT + (h % WIN) * WIN + w % WIN


def quad_index(h, w, rows, cols):
    pitch = pitch_of(cols // 2)
    return ((h % 2) + 2 * (w % 2)) * ((rows // 2) * pitch) + (h // 2) * pitch + w // 2


def ahead_index(h, w, ok, shift_rows, shift_cols, rows, cols, inner, base):
    pitch = pitch_of(cols)
    h2, w2 = h + shift_rows, w + shift_cols
    local = inner(jnp.minimum(h2, rows - 1), jnp.minimum(w2, cols - 1))
    below = base + (h2 - rows) * pitch + w2
    side = base + MARGIN * pitch + h2 * PM + (w2 - cols)
    idx = jnp.where(w2 >= cols, side, jnp.where(h2 >= rows, below, local))
    return jnp.where(ok, idx, -1).astype(jnp.int32).reshape(-1, 1)


def behind_index(h, w, ok, shift_rows, shift_cols, rows, cols, base):
    pitch = pitch_of(cols)
    h2, w2 = h - shift_rows, w - shift_cols
    local = win_index(jnp.maximum(h2, 0), jnp.maximum(w2, 0), cols)
    above = base + (h2 + MARGIN) * pitch + w2
    row = jnp.where(h2 >= 0, h2, rows + h2 + MARGIN)
    side = base + MARGIN * pitch + row * PM + (w2 + MARGIN)
    idx = jnp.where(w2 < 0, side, jnp.where(h2 < 0, above, local))
    return jnp.where(ok, idx, -1).astype(jnp.int32).reshape(-1, 1)


def piece_index(rows, cols, inner, first):
    top = 0 if first else rows - MARGIN
    left = 0 if first else cols - MARGIN
    parts = []
    for count, wide, pitch, h0, w0 in (
        (MARGIN, cols, pitch_of(cols), top, 0),
        (rows, MARGIN, PM, 0, left),
    ):
        h, w, ok = grid_tokens(count, wide, pitch)
        parts.append(np.where(ok, inner(h + h0, w + w0), -1))
    return np.concatenate(parts).astype(np.int32).reshape(-1, 1)


def window_labels(rows, cols, axis_row, axis_col, shift_rows, shift_cols):
    h, w, ok = window_tokens(rows, cols)
    height = rows * lax.axis_size("rows")
    breadth = cols * lax.axis_size("cols")
    gh = axis_row * rows + h
    gw = axis_col * cols + w
    lh = jnp.where(gh < height - WIN, 0, jnp.where(gh < height - shift_rows, 1, 2))
    lw = jnp.where(gw < breadth - WIN, 0, jnp.where(gw < breadth - shift_cols, 1, 2))
    flat = jnp.where(ok, lh * 3 + lw, -1).astype(jnp.int32)
    return flat.reshape(-1, 1), flat.reshape(-1, SLOT)


def dot(a, b):
    return jnp.dot(a, b, preferred_element_type=F32)


def dot_nt(a, b):
    return lax.dot_general(a, b, (((1,), (1,)), ((), ())), preferred_element_type=F32)


def dot_tn(a, b):
    return lax.dot_general(a, b, (((0,), (0,)), ((), ())), preferred_element_type=F32)


def select(idx, source):
    count = source.shape[0]
    lane = lax.broadcasted_iota(jnp.int32, (idx.shape[0], count), 1)
    hot = jnp.where(idx == lane, 1.0, 0.0).astype(BF16)
    return dot(hot, source).astype(BF16)


def norm_parts(x):
    centred = x - jnp.mean(x, axis=-1, keepdims=True)
    inverse = lax.rsqrt(jnp.mean(centred * centred, axis=-1, keepdims=True) + EPSILON)
    return centred * inverse, inverse


def norm_back(hat, inverse, gain, dy):
    grad_gain = jnp.sum(dy * hat, axis=0, keepdims=True)
    t = dy * gain
    dx = inverse * (
        t
        - jnp.mean(t, axis=-1, keepdims=True)
        - hat * jnp.mean(t * hat, axis=-1, keepdims=True)
    )
    return dx.astype(BF16), grad_gain


PACK = LANES // HEAD


def head_masks():
    lane = lax.broadcasted_iota(jnp.int32, (1, LANES), 1) // HEAD
    return [jnp.where(lane == h, 1.0, 0.0).astype(BF16) for h in range(PACK)]


def stack_heads(x, masks):
    return jnp.concatenate([x * m for m in masks], axis=0)


def pick_heads(o):
    lane = lax.broadcasted_iota(jnp.int32, (SLOT, LANES), 1) // HEAD
    out = o[:SLOT]
    for h in range(1, PACK):
        out = jnp.where(lane == h, o[h * SLOT : (h + 1) * SLOT], out)
    return out


def window_bias(lc_ref, lr_ref, w):
    lc = lc_ref[w * SLOT : (w + 1) * SLOT, :]
    lr = lr_ref[w : w + 1, :]
    bias = jnp.where((lc == lr) | (lc < 0), 0.0, MASKED)
    bias = jnp.where(lr < 0, -1e30, bias)
    return jnp.concatenate([bias] * PACK, axis=0)


def soft(qs, k, bias):
    raised = jnp.exp(dot_nt(qs, k) * HEAD ** (-0.5) + bias)
    return raised * (1.0 / jnp.sum(raised, axis=-1, keepdims=True))


def unit_back(qs, k, v, weights, wb, dm, masks):
    dms = stack_heads(dm, masks)
    dw = dot_nt(dms, v).astype(BF16).astype(F32)
    ds = weights * (dw - jnp.sum(dw * weights, axis=-1, keepdims=True))
    ds = (ds * HEAD ** (-0.5)).astype(BF16)
    dq = pick_heads(dot(ds, k))
    dk = dot_tn(ds, qs)
    dv = dot_tn(wb, dms)
    return dq.astype(BF16), dk.astype(BF16), dv.astype(BF16)


def fill_tile(scratch, tile, pitch):
    count, wide, _ = tile.shape
    for r in range(count):
        scratch[r * pitch : r * pitch + wide, :] = tile[r]


class Bag:
    pass


MESH = pl.DeviceIdType.MESH


class Links:
    def __init__(self, send, recv):
        self.send, self.recv, self.used = send, recv, 0
        self.group = lax.axis_index("groups")
        self.row, self.col = lax.axis_index("rows"), lax.axis_index("cols")
        self.nr, self.nc = lax.axis_size("rows"), lax.axis_size("cols")
        self.core, self.chip = lax.rem(self.col, 2), self.col // 2
        self.chips = self.nc // 2

    def device(self, dr, dc):
        row = lax.rem(self.row + dr + self.nr, self.nr)
        col = lax.rem(self.col + dc + self.nc, self.nc)
        return (self.group, row, col)

    def partner(self):
        return (self.group, self.row, self.chip * 2 + 1 - self.core)

    def barrier(self):
        offsets = {(d, 0) for d in range(1, self.nr)} | {(0, d) for d in range(1, self.nc)}
        offsets |= {(1, 1), (self.nr - 1, self.nc - 1)}
        sem = pltpu.get_barrier_semaphore()
        for dr, dc in sorted(offsets):
            pl.semaphore_signal(sem, inc=1, device_id=self.device(dr, dc), device_id_type=MESH)
        pl.semaphore_wait(sem, len(offsets))

    def start(self, source, target, device):
        copy = pltpu.make_async_remote_copy(
            src_ref=source,
            dst_ref=target,
            send_sem=self.send.at[self.used],
            recv_sem=self.recv.at[self.used],
            device_id=device,
            device_id_type=MESH,
        )
        self.used += 1
        copy.start()
        return copy

    def exchange(self, row, col, corner, halo, by):
        return [
            self.start(row, halo[0], self.device(by, 0)),
            self.start(col, halo[1], self.device(0, by)),
            self.start(corner, halo[2], self.device(by, by)),
        ]


def wait_all(copies):
    for copy in copies:
        copy.wait()


class Reduction:
    def __init__(self, links, kind, parts, bufs):
        self.links, self.kind, self.parts = links, kind, parts
        self.got1, self.half, self.got2, self.part, self.got3 = bufs

    def first(self):
        k = self.links
        self.copies = [k.start(self.parts.at[1 - k.core], self.got1, k.partner())]

    def second(self):
        k = self.links
        wait_all(self.copies)
        for x in range(k.chips):
            for r in range(k.nr):
                total = self.parts[k.core, x, r].astype(F32) + self.got1[x, r].astype(F32)
                self.half[x, r] = total.astype(self.kind)
        self.copies = [
            k.start(self.half.at[lax.rem(k.chip + d, k.chips)], self.got2.at[d - 1], k.device(0, 2 * d))
            for d in range(1, k.chips)
        ]

    def third(self):
        k = self.links
        wait_all(self.copies)
        for r in range(k.nr):
            total = self.half[k.chip, r].astype(F32)
            for d in range(1, k.chips):
                total = total + self.got2[d - 1, r].astype(F32)
            self.part[r] = total.astype(self.kind)
        self.copies = [
            k.start(self.part.at[lax.rem(k.row + d, k.nr)], self.got3.at[d - 1], k.device(d, 0))
            for d in range(1, k.nr)
        ]

    def finish(self):
        k = self.links
        wait_all(self.copies)
        total = self.part[k.row].astype(F32)
        for d in range(1, k.nr):
            total = total + self.got3[d - 1].astype(F32)
        return total


class GainSum:
    def __init__(self, links, bufs):
        self.links = links
        self.own, self.got1, self.half, self.got2, self.part, self.got3 = bufs

    def first(self):
        self.copies = [self.links.start(self.own, self.got1, self.links.partner())]

    def second(self):
        k = self.links
        wait_all(self.copies)
        self.half[...] = self.own[...] + self.got1[...]
        self.copies = [
            k.start(self.half, self.got2.at[d - 1], k.device(0, 2 * d)) for d in range(1, k.chips)
        ]

    def third(self):
        k = self.links
        wait_all(self.copies)
        total = self.half[...]
        for d in range(1, k.chips):
            total = total + self.got2[d - 1]
        self.part[...] = total
        self.copies = [k.start(self.part, self.got3.at[d - 1], k.device(d, 0)) for d in range(1, k.nr)]

    def finish(self):
        wait_all(self.copies)
        total = self.part[...]
        for d in range(1, self.links.nr):
            total = total + self.got3[d - 1]
        return total


def store_parts(parts, value, offset):
    _, chips, nr, depth, _ = parts.shape
    width = value.shape[1]
    for r in range(nr):
        for x in range(chips):
            for core in range(2):
                i = (r * chips + x) * 2 + core
                piece = value[i * depth : (i + 1) * depth]
                parts[core, x, r, :, offset : offset + width] = piece.astype(BF16)


def fill_side(scratch, tile):
    scratch[...] = jnp.zeros_like(scratch)
    for r in range(tile.shape[0]):
        scratch[r * PM : r * PM + MARGIN, :] = tile[r, :MARGIN, :]


def put_pieces(idx, source, row_ref, col_ref):
    got = select(idx[...], source)
    row_ref[...] = got[: row_ref.shape[0]]
    col_ref[...] = got[row_ref.shape[0] :]


def lanes_of(width, g):
    return [slice(t * width + g * LANES, t * width + (g + 1) * LANES) for t in range(3)]


def joined_ext(first, halo):
    return jnp.concatenate([first] + [h[...] for h in halo], axis=0)


def whole_kernel(in_names, out_names, scratch_names, *refs):
    b = Bag()
    for name, ref in zip(in_names + out_names + scratch_names, refs, strict=True):
        setattr(b, name, ref)
    links = Links(b.send, b.recv)
    rows, cols, narrow = b.tok.shape
    rows3, cols3, wide = b.cot.shape
    pitch, pitch3 = pitch_of(cols), pitch_of(cols3)
    red3 = Reduction(links, BF16, b.g3, [getattr(b, f"g3_{i}") for i in range(5)])
    redm = Reduction(links, BF16, b.gm, [getattr(b, f"gm_{i}") for i in range(5)])
    red2 = Reduction(links, BF16, b.g2, [getattr(b, f"g2_{i}") for i in range(5)])
    redg = GainSum(links, [getattr(b, f"gg_{i}") for i in range(6)])
    halos = [[getattr(b, f"h{n}_{i}") for i in range(3)] for n in range(7)]
    margin2 = slice(0, MARGIN * PM)
    masks = head_masks()

    b.toks[...] = jnp.zeros_like(b.toks)
    fill_tile(b.toks, b.tok, pitch)
    fill_side(b.tside, b.tok)
    b.cots[...] = jnp.zeros_like(b.cots)
    fill_tile(b.cots, b.cot, pitch3)
    fill_side(b.cside, b.cot)
    links.barrier()
    flying = links.exchange(
        b.toks.at[0 : MARGIN * pitch], b.tside, b.tside.at[margin2], halos[0], -1
    )
    flying_c = links.exchange(
        b.cots.at[0 : MARGIN * pitch3], b.cside, b.cside.at[margin2], halos[1], -1
    )

    quad = select(b.idx_q[...], b.toks[...])
    wait_all(flying)
    hat, _ = norm_parts(select(b.idx_a[...], joined_ext(b.toks[...], halos[0])).astype(F32))
    b.rolled[...] = (hat * b.gain2[...]).astype(BF16)
    b.packed[...] = dot(b.rolled[...], b.qkv2[...]).astype(BF16)
    for w in range(b.lr2.shape[0]):
        bias = window_bias(b.lc2, b.lr2, w)
        at = slice(w * SLOT, (w + 1) * SLOT)
        for g in range(narrow // LANES):
            lanes = lanes_of(narrow, g)
            qs = stack_heads(b.packed[at, lanes[0]], masks)
            wb = soft(qs, b.packed[at, lanes[1]], bias).astype(BF16)
            b.mixed[at, lanes[0]] = pick_heads(dot(wb, b.packed[at, lanes[2]])).astype(BF16)
    win = dot(b.mixed[...], b.proj2[...]).astype(BF16)
    put_pieces(b.idx_b, win, b.row1, b.col1)
    last2 = slice((rows - MARGIN) * PM, rows * PM)
    flying = links.exchange(b.row1, b.col1, b.col1.at[last2], halos[2], 1)

    wait_all(flying)
    restored = select(b.idx_c[...], joined_ext(win, halos[2]))
    section = (quad.astype(F32) + restored.astype(F32)).astype(BF16)
    t3 = rows3 * pitch3
    joined = jnp.concatenate([section[k * t3 : (k + 1) * t3] for k in range(4)], axis=1)
    b.joined[...] = joined
    hat, _ = norm_parts(joined.astype(F32))
    b.mnorm[...] = (hat * b.gainm[...]).astype(BF16)
    b.merged[...] = dot(b.mnorm[...], b.weight[...]).astype(BF16)
    hat, _ = norm_parts(b.merged[...].astype(F32))
    normed3 = (hat * b.gain3[...]).astype(BF16)
    b.normed3[...] = normed3
    for r in range(rows3):
        b.nside[r * PM : (r + 1) * PM, :] = normed3[r * pitch3 : r * pitch3 + PM]
    flying = links.exchange(
        b.normed3.at[0 : MARGIN * pitch3], b.nside, b.nside.at[margin2], halos[3], -1
    )

    wait_all(flying_c)
    dproj = select(b.idx_d[...], joined_ext(b.cots[...], halos[1]))
    dmixed = dot_nt(dproj, b.proj3[...]).astype(BF16)
    wait_all(flying)
    rolled3 = select(b.idx_d[...], joined_ext(b.normed3[...], halos[3]))
    b.packed3[...] = dot(rolled3, b.qkv3[...]).astype(BF16)
    for w in range(b.lr3.shape[0]):
        bias = window_bias(b.lc3, b.lr3, w)
        at = slice(w * SLOT, (w + 1) * SLOT)
        for g in range(wide // LANES):
            lanes = lanes_of(wide, g)
            qs = stack_heads(b.packed3[at, lanes[0]], masks)
            k, v = b.packed3[at, lanes[1]], b.packed3[at, lanes[2]]
            weights = soft(qs, k, bias)
            wb = weights.astype(BF16)
            b.mixed3[at, lanes[0]] = pick_heads(dot(wb, v)).astype(BF16)
            back = unit_back(qs, k, v, weights, wb, dmixed[at, lanes[0]], masks)
            for t in range(3):
                b.dpacked3[at, lanes[t]] = back[t]
    b.both[:, :wide] = dot(b.mixed3[...], b.proj3[...]).astype(BF16)
    b.both[:, wide:] = dot_nt(b.dpacked3[...], b.qkv3[...]).astype(BF16)
    put_pieces(b.idx_e, b.both[...], b.row2, b.col2)
    last3 = slice((rows3 - MARGIN) * PM, rows3 * PM)
    flying = links.exchange(b.row2, b.col2, b.col2.at[last3], halos[4], 1)
    store_parts(b.g3, dot_tn(rolled3, b.dpacked3[...]), 0)
    store_parts(b.g3, dot_tn(b.mixed3[...], dproj), 3 * wide)
    red3.first()

    wait_all(flying)
    back = select(b.idx_f[...], joined_ext(b.both[...], halos[4]))
    mine = b.merged[...].astype(F32)
    total = (mine + back[:, :wide].astype(F32)).astype(BF16)
    for r in range(rows3):
        b.out[r] = total[r * pitch3 : r * pitch3 + cols3]
    hat, inv = norm_parts(mine)
    dmerged, grad3 = norm_back(hat, inv, b.gain3[...], back[:, wide:].astype(F32))
    dmerged = b.cots[...] + dmerged
    hat, inv = norm_parts(b.joined[...].astype(F32))
    djn = dot_nt(dmerged, b.weight[...]).astype(BF16).astype(F32)
    djoined, gradm = norm_back(hat, inv, b.gainm[...], djn)
    b.gg_0[:, narrow : 5 * narrow] = gradm
    b.gg_0[:, 5 * narrow :] = grad3
    b.dsec[...] = jnp.concatenate(
        [djoined[:, k * narrow : (k + 1) * narrow] for k in range(4)], axis=0
    )
    put_pieces(b.idx_g, b.dsec[...], b.row3, b.col3)
    flying = links.exchange(b.row3, b.col3, b.col3.at[margin2], halos[5], -1)
    store_parts(b.gm, dot_tn(b.mnorm[...], dmerged), 0)
    redm.first()

    wait_all(flying)
    red3.second()
    dproj = select(b.idx_h[...], joined_ext(b.dsec[...], halos[5]))
    dmixed = dot_nt(dproj, b.proj2[...]).astype(BF16)
    for w in range(b.lr2.shape[0]):
        bias = window_bias(b.lc2, b.lr2, w)
        at = slice(w * SLOT, (w + 1) * SLOT)
        for g in range(narrow // LANES):
            lanes = lanes_of(narrow, g)
            qs = stack_heads(b.packed[at, lanes[0]], masks)
            k, v = b.packed[at, lanes[1]], b.packed[at, lanes[2]]
            weights = soft(qs, k, bias)
            back = unit_back(
                qs, k, v, weights, weights.astype(BF16), dmixed[at, lanes[0]], masks
            )
            for t in range(3):
                b.dpacked[at, lanes[t]] = back[t]
    drolled = dot_nt(b.dpacked[...], b.qkv2[...]).astype(BF16)
    put_pieces(b.idx_b, drolled, b.row4, b.col4)
    flying = links.exchange(b.row4, b.col4, b.col4.at[last2], halos[6], 1)
    store_parts(b.g2, dot_tn(b.rolled[...], b.dpacked[...]), 0)
    store_parts(b.g2, dot_tn(b.mixed[...], dproj), 3 * narrow)
    red2.first()
    red3.third()
    redm.second()

    wait_all(flying)
    dnormed = select(b.idx_i[...], joined_ext(drolled, halos[6])).astype(F32)
    hat, inv = norm_parts(b.toks[...].astype(F32))
    dtok, grad2 = norm_back(hat, inv, b.gain2[...], dnormed)
    b.gg_0[:, :narrow] = grad2
    redg.first()
    red2.second()
    total = select(b.idx_n[...], b.dsec[...]) + dtok
    for r in range(rows):
        b.dtok[r] = total[r * pitch : r * pitch + cols]
    redg.second()
    redm.third()
    red2.third()
    redg.third()
    b.sum3[...] = red3.finish().astype(BF16)
    b.summ[...] = redm.finish().astype(BF16)
    b.sum2[...] = red2.finish().astype(BF16)
    b.gains[...] = redg.finish()


def on_device(
    tokens, cotangent, shifts, norm2_gain, qkv2, proj2, merge_gain, merge_weight, norm3_gain,
    qkv3, proj3,
):
    rows, cols, narrow = tokens.shape
    wide = qkv3.shape[0]
    rows3, cols3 = rows // 2, cols // 2
    pitch, pitch3 = pitch_of(cols), pitch_of(cols3)
    base, base3 = rows * pitch, rows3 * pitch3
    r, c = lax.axis_index("rows"), lax.axis_index("cols")
    s0, s1, s2, s3 = shifts[0], shifts[1], shifts[2], shifts[3]

    win2, win3 = window_tokens(rows, cols), window_tokens(rows3, cols3)
    n2, n3 = len(win2[0]), len(win3[0])
    quad = quad_tokens(rows, cols)
    nat = grid_tokens(rows, cols, pitch)
    grid3 = grid_tokens(rows3, cols3, pitch3)
    as_grid = lambda h, w: h * pitch + w
    as_grid3 = lambda h, w: h * pitch3 + w
    as_quad = lambda h, w: quad_index(h, w, rows, cols)
    as_win = lambda h, w: win_index(h, w, cols)
    as_win3 = lambda h, w: win_index(h, w, cols3)
    fixed = lambda t, inner: np.where(t[2], inner(t[0], t[1]), -1).astype(np.int32).reshape(-1, 1)

    idx_a = ahead_index(*win2, s0, s1, rows, cols, as_grid, base)
    idx_h = ahead_index(*win2, s0, s1, rows, cols, as_quad, len(quad[0]))
    idx_d = ahead_index(*win3, s2, s3, rows3, cols3, as_grid3, base3)
    idx_c = behind_index(*quad, s0, s1, rows, cols, n2)
    idx_i = behind_index(*nat, s0, s1, rows, cols, n2)
    idx_f = behind_index(*grid3, s2, s3, rows3, cols3, n3)
    idx_q = fixed(quad, as_grid)
    idx_n = fixed(nat, as_quad)
    idx_b = piece_index(rows, cols, as_win, False)
    idx_e = piece_index(rows3, cols3, as_win3, False)
    idx_g = piece_index(rows, cols, as_quad, True)
    lc2, lr2 = window_labels(rows, cols, r, c, s0, s1)
    lc3, lr3 = window_labels(rows3, cols3, r, c, s2, s3)
    gain2, gainm, gain3 = (g.reshape(1, -1) for g in (norm2_gain, merge_gain, norm3_gain))
    nr, nc = lax.axis_size("rows"), lax.axis_size("cols")
    chips = nc // 2
    quads, gains = len(quad[0]), 5 * narrow + wide
    inputs = dict(
        tok=tokens, cot=cotangent, idx_a=idx_a, idx_b=idx_b, idx_c=idx_c, idx_d=idx_d, idx_e=idx_e,
        idx_f=idx_f, idx_g=idx_g, idx_h=idx_h, idx_i=idx_i, idx_n=idx_n, idx_q=idx_q, lc2=lc2,
        lr2=lr2, lc3=lc3, lr3=lr3, gain2=gain2, gainm=gainm, gain3=gain3, qkv2=qkv2, proj2=proj2,
        weight=merge_weight, qkv3=qkv3, proj3=proj3,
    )
    m3, mm, m2 = wide // (nr * nc), 4 * narrow // (nr * nc), narrow // (nr * nc)
    outs = dict(
        out=(cotangent.shape, BF16),
        dtok=(tokens.shape, BF16),
        gains=((1, gains), F32),
        sum3=((m3, 4 * wide), BF16),
        summ=((mm, wide), BF16),
        sum2=((m2, 4 * narrow), BF16),
    )
    row2, col2, cor = MARGIN * pitch, rows * PM, MARGIN * PM
    row3, col3 = MARGIN * pitch3, rows3 * PM
    scratch = dict(
        toks=((base, narrow), BF16), tside=((col2, narrow), BF16),
        cots=((base3, wide), BF16), cside=((col3, wide), BF16),
        rolled=((n2, narrow), BF16), packed=((n2, 3 * narrow), BF16), mixed=((n2, narrow), BF16),
        joined=((base3, 4 * narrow), BF16), mnorm=((base3, 4 * narrow), BF16),
        merged=((base3, wide), BF16), normed3=((base3, wide), BF16), nside=((col3, wide), BF16),
        packed3=((n3, 3 * wide), BF16), mixed3=((n3, wide), BF16),
        dpacked3=((n3, 3 * wide), BF16), both=((n3, 2 * wide), BF16),
        dsec=((quads, narrow), BF16), dpacked=((n2, 3 * narrow), BF16),
        row1=((row2, narrow), BF16), col1=((col2, narrow), BF16),
        row2=((row3, 2 * wide), BF16), col2=((col3, 2 * wide), BF16),
        row3=((row2, narrow), BF16), col3=((col2, narrow), BF16),
        row4=((row2, narrow), BF16), col4=((col2, narrow), BF16),
    )
    copies = 7 * 3
    for n, (big, width) in enumerate(
        ((1, narrow), (0, wide), (1, narrow), (0, wide), (0, 2 * wide), (1, narrow), (1, narrow))
    ):
        for i, size in enumerate((row2, col2, cor) if big else (row3, col3, cor)):
            scratch[f"h{n}_{i}"] = ((size, width), BF16)
    for name, shape in (("g3", (m3, 4 * wide)), ("gm", (mm, wide)), ("g2", (m2, 4 * narrow))):
        scratch[name] = ((2, chips, nr) + shape, BF16)
        for i, lead in enumerate(
            ((chips, nr), (chips, nr), (max(chips - 1, 1), nr), (nr,), (max(nr - 1, 1),))
        ):
            scratch[f"{name}_{i}"] = (lead + shape, BF16)
        copies += chips + nr - 1
    for i, lead in enumerate(((), (), (), (max(chips - 1, 1),), (), (max(nr - 1, 1),))):
        scratch[f"gg_{i}"] = (lead + (1, gains), F32)
    copies += chips + nr - 1
    spaces = [pltpu.VMEM(s, d) for s, d in scratch.values()]
    spaces += [pltpu.SemaphoreType.DMA((copies,)), pltpu.SemaphoreType.DMA((copies,))]
    out, tokens_grad, total, sum3, sum_m, sum2 = pl.pallas_call(
        functools.partial(
            whole_kernel, list(inputs), list(outs), list(scratch) + ["send", "recv"]
        ),
        out_shape=[jax.ShapeDtypeStruct(s, d) for s, d in outs.values()],
        in_specs=[pl.BlockSpec(memory_space=pltpu.VMEM)] * len(inputs),
        out_specs=[pl.BlockSpec(memory_space=pltpu.VMEM)] * len(outs),
        scratch_shapes=spaces,
        compiler_params=pltpu.CompilerParams(
            collective_id=0, has_side_effects=True, vmem_limit_bytes=60 * 2**20
        ),
        name="block",
    )(*inputs.values())
    return (
        out,
        tokens_grad,
        total.reshape(-1),
        sum2[:, : 3 * narrow].reshape(-1),
        sum2[:, 3 * narrow :].reshape(-1),
        sum_m.reshape(-1),
        sum3[:, : 3 * wide].reshape(-1),
        sum3[:, 3 * wide :].reshape(-1),
    )


def solution(mesh):
    tile = P(("groups", "rows"), "cols", None)
    spread = P(("groups", "rows", "cols"))
    return jax.shard_map(
        on_device,
        mesh=mesh,
        in_specs=(tile, tile) + (P(),) * 9,
        out_specs=(tile, tile, P("groups")) + (spread,) * 5,
        check_vma=False,
    )
```

```python
import functools

import jax
import jax.numpy as jnp
import numpy as np
from jax import lax
from jax.experimental import pallas as pl
from jax.experimental.pallas import tpu as pltpu
from jax.sharding import PartitionSpec as P

HEAD = 32
WIN = 7
MARGIN = WIN - 1
SLOT = 64
PM = 16
LANES = 128
EPSILON = 1e-05
MASKED = -100.0
F32 = jnp.float32
BF16 = jnp.bfloat16


def pitch_of(count):
    return -(-count // 16) * 16


def window_tokens(rows, cols):
    h, w, ok = [], [], []
    for wr in range(rows // WIN):
        for wc in range(cols // WIN):
            for t in range(SLOT):
                good = t < WIN * WIN
                h.append(wr * WIN + t // WIN if good else 0)
                w.append(wc * WIN + t % WIN if good else 0)
                ok.append(good)
    return np.array(h, np.int32), np.array(w, np.int32), np.array(ok)


def grid_tokens(rows, cols, pitch):
    h = np.repeat(np.arange(rows, dtype=np.int32), pitch)
    w = np.tile(np.arange(pitch, dtype=np.int32), rows)
    ok = w < cols
    return h, np.where(ok, w, 0).astype(np.int32), ok


def quad_tokens(rows, cols):
    a, b, ok = grid_tokens(rows // 2, cols // 2, pitch_of(cols // 2))
    h = np.concatenate([2 * a + (k & 1) for k in range(4)])
    w = np.concatenate([2 * b + (k >> 1) for k in range(4)])
    return h, w, np.tile(ok, 4)


def by_window(x):
    return (x * 9363) >> 16


def win_index(h, w, cols):
    hq, wq = by_window(h), by_window(w)
    return (hq * (cols // WIN) + wq) * SLOT + (h - hq * WIN) * WIN + w - wq * WIN


def quad_index(h, w, rows, cols):
    pitch = pitch_of(cols // 2)
    return ((h & 1) + 2 * (w & 1)) * ((rows // 2) * pitch) + (h >> 1) * pitch + (w >> 1)


def coded(tokens):
    h, w, ok = tokens
    return np.where(ok, h * 4096 + w, -1).astype(np.int32).reshape(-1, 1)


def decoded(code):
    return code >> 12, code & 4095, code >= 0


def ahead_index(code, shift_rows, shift_cols, rows, cols, inner, base):
    h, w, ok = decoded(code)
    pitch = pitch_of(cols)
    h2, w2 = h + shift_rows, w + shift_cols
    local = inner(jnp.minimum(h2, rows - 1), jnp.minimum(w2, cols - 1))
    below = base + (h2 - rows) * pitch + w2
    side = base + MARGIN * pitch + h2 * PM + (w2 - cols)
    return jnp.where(ok, jnp.where(w2 >= cols, side, jnp.where(h2 >= rows, below, local)), -1)


def behind_index(code, shift_rows, shift_cols, rows, cols, base):
    h, w, ok = decoded(code)
    pitch = pitch_of(cols)
    h2, w2 = h - shift_rows, w - shift_cols
    local = win_index(jnp.maximum(h2, 0), jnp.maximum(w2, 0), cols)
    above = base + (h2 + MARGIN) * pitch + w2
    row = jnp.where(h2 >= 0, h2, rows + h2 + MARGIN)
    side = base + MARGIN * pitch + row * PM + (w2 + MARGIN)
    return jnp.where(ok, jnp.where(w2 < 0, side, jnp.where(h2 < 0, above, local)), -1)


def piece_index(rows, cols, inner, first):
    top = 0 if first else rows - MARGIN
    left = 0 if first else cols - MARGIN
    parts = []
    for count, wide, pitch, h0, w0 in (
        (MARGIN, cols, pitch_of(cols), top, 0),
        (rows, MARGIN, PM, 0, left),
    ):
        h, w, ok = grid_tokens(count, wide, pitch)
        parts.append(np.where(ok, inner(h + h0, w + w0), -1))
    return np.concatenate(parts).astype(np.int32).reshape(-1, 1)


def window_labels(code, rows, cols, axis_row, axis_col, shift_rows, shift_cols):
    h, w, ok = decoded(code)
    height = rows * lax.axis_size("rows")
    breadth = cols * lax.axis_size("cols")
    gh = axis_row * rows + h
    gw = axis_col * cols + w
    lh = jnp.where(gh < height - WIN, 0, jnp.where(gh < height - shift_rows, 1, 2))
    lw = jnp.where(gw < breadth - WIN, 0, jnp.where(gw < breadth - shift_cols, 1, 2))
    return jnp.where(ok, lh * 3 + lw, -1)


def dot(a, b):
    return jnp.dot(a, b, preferred_element_type=F32)


def dot_nt(a, b):
    return lax.dot_general(a, b, (((1,), (1,)), ((), ())), preferred_element_type=F32)


def dot_tn(a, b):
    return lax.dot_general(a, b, (((0,), (0,)), ((), ())), preferred_element_type=F32)


def one_hot(idx, count):
    lane = lax.broadcasted_iota(jnp.int32, (idx.shape[0], count), 1)
    return jnp.where(idx == lane, 1.0, 0.0).astype(BF16)


def picked(hot, source):
    return dot(hot, source).astype(BF16)


def select(idx, source):
    return picked(one_hot(idx, source.shape[0]), source)


def norm_parts(x):
    centred = x - jnp.mean(x, axis=-1, keepdims=True)
    inverse = lax.rsqrt(jnp.mean(centred * centred, axis=-1, keepdims=True) + EPSILON)
    return centred * inverse, inverse


def norm_back(hat, inverse, gain, dy):
    grad_gain = jnp.sum(dy * hat, axis=0, keepdims=True)
    t = dy * gain
    dx = inverse * (
        t
        - jnp.mean(t, axis=-1, keepdims=True)
        - hat * jnp.mean(t * hat, axis=-1, keepdims=True)
    )
    return dx.astype(BF16), grad_gain


PACK = LANES // HEAD


def head_masks():
    lane = lax.broadcasted_iota(jnp.int32, (1, LANES), 1) // HEAD
    return [jnp.where(lane == h, 1.0, 0.0).astype(BF16) for h in range(PACK)]


def stack_heads(x, masks):
    return jnp.concatenate([x * m for m in masks], axis=0)


def pick_heads(o):
    lane = lax.broadcasted_iota(jnp.int32, (SLOT, LANES), 1) // HEAD
    out = o[:SLOT]
    for h in range(1, PACK):
        out = jnp.where(lane == h, o[h * SLOT : (h + 1) * SLOT], out)
    return out


def window_bias(lc_ref, lr_ref, w):
    lc = lc_ref[w * SLOT : (w + 1) * SLOT, :]
    lr = lr_ref[w : w + 1, :]
    bias = jnp.where((lc == lr) | (lc < 0), 0.0, MASKED)
    bias = jnp.where(lr < 0, -1e30, bias)
    return jnp.concatenate([bias] * PACK, axis=0)


def soft(qs, k, bias):
    raised = jnp.exp(dot_nt(qs, k) * HEAD ** (-0.5) + bias)
    return raised * (1.0 / jnp.sum(raised, axis=-1, keepdims=True))


def unit_back(qs, k, v, weights, wb, dm, masks):
    dms = stack_heads(dm, masks)
    dw = dot_nt(dms, v).astype(BF16).astype(F32)
    ds = weights * (dw - jnp.sum(dw * weights, axis=-1, keepdims=True))
    ds = (ds * HEAD ** (-0.5)).astype(BF16)
    dq = pick_heads(dot(ds, k))
    dk = dot_tn(ds, qs)
    dv = dot_tn(wb, dms)
    return dq.astype(BF16), dk.astype(BF16), dv.astype(BF16)


def fill_tile(scratch, tile, pitch):
    count, wide, _ = tile.shape
    for r in range(count):
        scratch[r * pitch : r * pitch + wide, :] = tile[r]


class Bag:
    pass


MESH = pl.DeviceIdType.MESH


class Links:
    def __init__(self, send, recv):
        self.send, self.recv, self.used = send, recv, 0
        self.group = lax.axis_index("groups")
        self.row, self.col = lax.axis_index("rows"), lax.axis_index("cols")
        self.nr, self.nc = lax.axis_size("rows"), lax.axis_size("cols")
        self.core, self.chip = lax.rem(self.col, 2), self.col // 2
        self.chips = self.nc // 2

    def device(self, dr, dc):
        row = lax.rem(self.row + dr + self.nr, self.nr)
        col = lax.rem(self.col + dc + self.nc, self.nc)
        return (self.group, row, col)

    def partner(self):
        return (self.group, self.row, self.chip * 2 + 1 - self.core)

    def barrier(self):
        offsets = {(d, 0) for d in range(1, self.nr)} | {(0, d) for d in range(1, self.nc)}
        offsets |= {(1, 1), (self.nr - 1, self.nc - 1)}
        sem = pltpu.get_barrier_semaphore()
        for dr, dc in sorted(offsets):
            pl.semaphore_signal(sem, inc=1, device_id=self.device(dr, dc), device_id_type=MESH)
        pl.semaphore_wait(sem, len(offsets))

    def start(self, source, target, device):
        copy = pltpu.make_async_remote_copy(
            src_ref=source,
            dst_ref=target,
            send_sem=self.send.at[self.used],
            recv_sem=self.recv.at[self.used],
            device_id=device,
            device_id_type=MESH,
        )
        self.used += 1
        copy.start()
        return copy

    def exchange(self, row, col, corner, halo, by):
        return [
            self.start(row, halo[0], self.device(by, 0)),
            self.start(col, halo[1], self.device(0, by)),
            self.start(corner, halo[2], self.device(by, by)),
        ]


def wait_all(copies):
    for copy in copies:
        copy.wait()


class Reduction:
    def __init__(self, links, kind, parts, bufs):
        self.links, self.kind, self.parts = links, kind, parts
        self.got1, self.half, self.got2, self.part, self.got3 = bufs

        self.copies = []

    def first(self, chips=None):
        k = self.links
        for x in range(k.chips) if chips is None else chips:
            self.copies.append(
                k.start(self.parts.at[1 - k.core, x], self.got1.at[x], k.partner())
            )

    def second(self):
        k = self.links
        wait_all(self.copies)
        for x in range(k.chips):
            for r in range(k.nr):
                total = self.parts[k.core, x, r].astype(F32) + self.got1[x, r].astype(F32)
                self.half[x, r] = total.astype(self.kind)
        self.copies = [
            k.start(self.half.at[lax.rem(k.chip + d, k.chips)], self.got2.at[d - 1], k.device(0, 2 * d))
            for d in range(1, k.chips)
        ]

    def third(self):
        k = self.links
        wait_all(self.copies)
        for r in range(k.nr):
            total = self.half[k.chip, r].astype(F32)
            for d in range(1, k.chips):
                total = total + self.got2[d - 1, r].astype(F32)
            self.part[r] = total.astype(self.kind)
        self.copies = [
            k.start(self.part.at[lax.rem(k.row + d, k.nr)], self.got3.at[d - 1], k.device(d, 0))
            for d in range(1, k.nr)
        ]

    def finish(self):
        k = self.links
        wait_all(self.copies)
        total = self.part[k.row].astype(F32)
        for d in range(1, k.nr):
            total = total + self.got3[d - 1].astype(F32)
        return total


class GainSum:
    def __init__(self, links, bufs):
        self.links = links
        self.own, self.got1, self.half, self.got2, self.part, self.got3 = bufs

    def first(self):
        self.copies = [self.links.start(self.own, self.got1, self.links.partner())]

    def second(self):
        k = self.links
        wait_all(self.copies)
        self.half[...] = self.own[...] + self.got1[...]
        self.copies = [
            k.start(self.half, self.got2.at[d - 1], k.device(0, 2 * d)) for d in range(1, k.chips)
        ]

    def third(self):
        k = self.links
        wait_all(self.copies)
        total = self.half[...]
        for d in range(1, k.chips):
            total = total + self.got2[d - 1]
        self.part[...] = total
        self.copies = [k.start(self.part, self.got3.at[d - 1], k.device(d, 0)) for d in range(1, k.nr)]

    def finish(self):
        wait_all(self.copies)
        total = self.part[...]
        for d in range(1, self.links.nr):
            total = total + self.got3[d - 1]
        return total


def store_parts(parts, value, offset):
    _, chips, nr, depth, _ = parts.shape
    width = value.shape[1]
    for r in range(nr):
        for x in range(chips):
            for core in range(2):
                i = (r * chips + x) * 2 + core
                piece = value[i * depth : (i + 1) * depth]
                parts[core, x, r, :, offset : offset + width] = piece.astype(BF16)


def fill_side(scratch, tile):
    scratch[...] = jnp.zeros_like(scratch)
    for r in range(tile.shape[0]):
        scratch[r * PM : r * PM + MARGIN, :] = tile[r, :MARGIN, :]


def put_pieces(idx, source, row_ref, col_ref):
    got = select(idx[...], source)
    row_ref[...] = got[: row_ref.shape[0]]
    col_ref[...] = got[row_ref.shape[0] :]


def lanes_of(width, g):
    return [slice(t * width + g * LANES, t * width + (g + 1) * LANES) for t in range(3)]


def joined_ext(first, halo):
    return jnp.concatenate([first] + [h[...] for h in halo], axis=0)


def whole_kernel(in_names, out_names, scratch_names, *refs):
    b = Bag()
    for name, ref in zip(in_names + out_names + scratch_names, refs, strict=True):
        setattr(b, name, ref)
    links = Links(b.send, b.recv)
    rows, cols, narrow = b.tok.shape
    rows3, cols3, wide = b.cot.shape
    pitch, pitch3 = pitch_of(cols), pitch_of(cols3)
    red3 = Reduction(links, BF16, b.g3, [getattr(b, f"g3_{i}") for i in range(5)])
    redm = Reduction(links, BF16, b.gm, [getattr(b, f"gm_{i}") for i in range(5)])
    red2 = Reduction(links, BF16, b.g2, [getattr(b, f"g2_{i}") for i in range(5)])
    redg = GainSum(links, [getattr(b, f"gg_{i}") for i in range(6)])
    halos = [[getattr(b, f"h{n}_{i}") for i in range(3)] for n in range(7)]
    margin2 = slice(0, MARGIN * PM)
    masks = head_masks()
    s0, s1, s2, s3 = (b.shifts[i] for i in range(4))
    quads, quad_pitch = b.quad.shape[0], pitch_of(cols // 2)
    n2, n3 = b.win2.shape[0], b.win3.shape[0]
    base, base3 = rows * pitch, rows3 * pitch3
    as_grid = lambda h, w: h * pitch + w
    as_grid3 = lambda h, w: h * pitch3 + w
    as_quad = lambda h, w: quad_index(h, w, rows, cols)
    extra = MARGIN * pitch + (rows + MARGIN) * PM
    extra3 = MARGIN * pitch3 + (rows3 + MARGIN) * PM

    b.toks[...] = jnp.zeros_like(b.toks)
    fill_tile(b.toks, b.tok, pitch)
    fill_side(b.tside, b.tok)
    b.cots[...] = jnp.zeros_like(b.cots)
    fill_tile(b.cots, b.cot, pitch3)
    fill_side(b.cside, b.cot)
    links.barrier()
    flying = links.exchange(
        b.toks.at[0 : MARGIN * pitch], b.tside, b.tside.at[margin2], halos[0], -1
    )
    flying_c = links.exchange(
        b.cots.at[0 : MARGIN * pitch3], b.cside, b.cside.at[margin2], halos[1], -1
    )

    place2 = (rows, cols, links.row, links.col, s0, s1)
    place3 = (rows3, cols3, links.row, links.col, s2, s3)
    b.lc2[...] = window_labels(b.win2[...], *place2)
    b.lr2[...] = window_labels(b.rwin2[...], *place2)
    b.lc3[...] = window_labels(b.win3[...], *place3)
    b.lr3[...] = window_labels(b.rwin3[...], *place3)
    quad = select(b.idx_q[...], b.toks[...])
    idx = ahead_index(b.win2[...], s0, s1, rows, cols, as_grid, base)
    hot = one_hot(idx, base + extra)
    wait_all(flying)
    hat, _ = norm_parts(picked(hot, joined_ext(b.toks[...], halos[0])).astype(F32))
    b.rolled[...] = (hat * b.gain2[...]).astype(BF16)
    b.packed[...] = dot(b.rolled[...], b.qkv2[...]).astype(BF16)
    for w in range(b.lr2.shape[0]):
        bias = window_bias(b.lc2, b.lr2, w)
        at = slice(w * SLOT, (w + 1) * SLOT)
        for g in range(narrow // LANES):
            lanes = lanes_of(narrow, g)
            qs = stack_heads(b.packed[at, lanes[0]], masks)
            wb = soft(qs, b.packed[at, lanes[1]], bias).astype(BF16)
            b.mixed[at, lanes[0]] = pick_heads(dot(wb, b.packed[at, lanes[2]])).astype(BF16)
    win = dot(b.mixed[...], b.proj2[...]).astype(BF16)
    put_pieces(b.idx_b, win, b.row1, b.col1)
    last2 = slice((rows - MARGIN) * PM, rows * PM)
    flying = links.exchange(b.row1, b.col1, b.col1.at[last2], halos[2], 1)

    hot = one_hot(behind_index(b.quad[...], s0, s1, rows, cols, n2), n2 + extra)
    wait_all(flying)
    restored = picked(hot, joined_ext(win, halos[2]))
    section = (quad.astype(F32) + restored.astype(F32)).astype(BF16)
    t3 = rows3 * pitch3
    joined = jnp.concatenate([section[k * t3 : (k + 1) * t3] for k in range(4)], axis=1)
    b.joined[...] = joined
    hat, _ = norm_parts(joined.astype(F32))
    b.mnorm[...] = (hat * b.gainm[...]).astype(BF16)
    b.merged[...] = dot(b.mnorm[...], b.weight[...]).astype(BF16)
    hat, _ = norm_parts(b.merged[...].astype(F32))
    normed3 = (hat * b.gain3[...]).astype(BF16)
    b.normed3[...] = normed3
    for r in range(rows3):
        b.nside[r * PM : (r + 1) * PM, :] = normed3[r * pitch3 : r * pitch3 + PM]
    flying = links.exchange(
        b.normed3.at[0 : MARGIN * pitch3], b.nside, b.nside.at[margin2], halos[3], -1
    )

    wait_all(flying_c)
    idx = ahead_index(b.win3[...], s2, s3, rows3, cols3, as_grid3, base3)
    hot = one_hot(idx, base3 + extra3)
    dproj = picked(hot, joined_ext(b.cots[...], halos[1]))
    dmixed = dot_nt(dproj, b.proj3[...]).astype(BF16)
    wait_all(flying)
    rolled3 = picked(hot, joined_ext(b.normed3[...], halos[3]))
    b.packed3[...] = dot(rolled3, b.qkv3[...]).astype(BF16)
    for w in range(b.lr3.shape[0]):
        bias = window_bias(b.lc3, b.lr3, w)
        at = slice(w * SLOT, (w + 1) * SLOT)
        for g in range(wide // LANES):
            lanes = lanes_of(wide, g)
            qs = stack_heads(b.packed3[at, lanes[0]], masks)
            k, v = b.packed3[at, lanes[1]], b.packed3[at, lanes[2]]
            weights = soft(qs, k, bias)
            wb = weights.astype(BF16)
            b.mixed3[at, lanes[0]] = pick_heads(dot(wb, v)).astype(BF16)
            back = unit_back(qs, k, v, weights, wb, dmixed[at, lanes[0]], masks)
            for t in range(3):
                b.dpacked3[at, lanes[t]] = back[t]
    b.both[:, :wide] = dot(b.mixed3[...], b.proj3[...]).astype(BF16)
    b.both[:, wide:] = dot_nt(b.dpacked3[...], b.qkv3[...]).astype(BF16)
    put_pieces(b.idx_e, b.both[...], b.row2, b.col2)
    last3 = slice((rows3 - MARGIN) * PM, rows3 * PM)
    flying = links.exchange(b.row2, b.col2, b.col2.at[last3], halos[4], 1)
    store_parts(b.g3, dot_tn(rolled3, b.dpacked3[...]), 0)
    store_parts(b.g3, dot_tn(b.mixed3[...], dproj), 3 * wide)
    red3.first(range(links.chips // 2))

    hot = one_hot(behind_index(b.grid3[...], s2, s3, rows3, cols3, n3), n3 + extra3)
    wait_all(flying)
    back = picked(hot, joined_ext(b.both[...], halos[4]))
    mine = b.merged[...].astype(F32)
    total = (mine + back[:, :wide].astype(F32)).astype(BF16)
    for r in range(rows3):
        b.out[r] = total[r * pitch3 : r * pitch3 + cols3]
    hat, inv = norm_parts(mine)
    dmerged, grad3 = norm_back(hat, inv, b.gain3[...], back[:, wide:].astype(F32))
    dmerged = b.cots[...] + dmerged
    hat, inv = norm_parts(b.joined[...].astype(F32))
    djn = dot_nt(dmerged, b.weight[...]).astype(BF16).astype(F32)
    djoined, gradm = norm_back(hat, inv, b.gainm[...], djn)
    b.gg_0[:, narrow : 5 * narrow] = gradm
    b.gg_0[:, 5 * narrow :] = grad3
    b.dsec[...] = jnp.concatenate(
        [djoined[:, k * narrow : (k + 1) * narrow] for k in range(4)], axis=0
    )
    put_pieces(b.idx_g, b.dsec[...], b.row3, b.col3)
    flying = links.exchange(b.row3, b.col3, b.col3.at[margin2], halos[5], -1)
    red3.first(range(links.chips // 2, links.chips))
    store_parts(b.gm, dot_tn(b.mnorm[...], dmerged), 0)
    redm.first()

    idx = ahead_index(b.win2[...], s0, s1, rows, cols, as_quad, quads)
    hot = one_hot(idx, quads + extra)
    wait_all(flying)
    dproj = picked(hot, joined_ext(b.dsec[...], halos[5]))
    dmixed = dot_nt(dproj, b.proj2[...]).astype(BF16)
    for w in range(b.lr2.shape[0]):
        if w == b.lr2.shape[0] // 2:
            red3.second()
        bias = window_bias(b.lc2, b.lr2, w)
        at = slice(w * SLOT, (w + 1) * SLOT)
        for g in range(narrow // LANES):
            lanes = lanes_of(narrow, g)
            qs = stack_heads(b.packed[at, lanes[0]], masks)
            k, v = b.packed[at, lanes[1]], b.packed[at, lanes[2]]
            weights = soft(qs, k, bias)
            back = unit_back(
                qs, k, v, weights, weights.astype(BF16), dmixed[at, lanes[0]], masks
            )
            for t in range(3):
                b.dpacked[at, lanes[t]] = back[t]
    drolled = dot_nt(b.dpacked[...], b.qkv2[...]).astype(BF16)
    put_pieces(b.idx_b, drolled, b.row4, b.col4)
    flying = links.exchange(b.row4, b.col4, b.col4.at[last2], halos[6], 1)
    store_parts(b.g2, dot_tn(b.rolled[...], b.dpacked[...]), 0)
    store_parts(b.g2, dot_tn(b.mixed[...], dproj), 3 * narrow)
    red2.first()
    red3.third()
    redm.second()

    hot = one_hot(behind_index(b.nat[...], s0, s1, rows, cols, n2), n2 + extra)
    wait_all(flying)
    dnormed = picked(hot, joined_ext(drolled, halos[6])).astype(F32)
    hat, inv = norm_parts(b.toks[...].astype(F32))
    dtok, grad2 = norm_back(hat, inv, b.gain2[...], dnormed)
    b.gg_0[:, :narrow] = grad2
    redg.first()
    red2.second()
    total = select(b.idx_n[...], b.dsec[...]) + dtok
    for r in range(rows):
        b.dtok[r] = total[r * pitch : r * pitch + cols]
    redg.second()
    redm.third()
    red2.third()
    redg.third()
    b.sum3[...] = red3.finish().astype(BF16)
    b.summ[...] = redm.finish().astype(BF16)
    b.sum2[...] = red2.finish().astype(BF16)
    b.gains[...] = redg.finish()


def finish_kernel(out, dtok, gains, sum3, summ, sum2, o_out, o_dtok, o_gains, *rest):
    o_out[...] = out[...]
    o_dtok[...] = dtok[...]
    for j in range(o_gains.shape[0]):
        o_gains[j : j + 1, :] = gains[:, j * LANES : (j + 1) * LANES]
    flats, rooms = rest[: len(rest) // 2], rest[len(rest) // 2 :]
    wide, narrow = sum3.shape[1] // 4, sum2.shape[1] // 4
    views = (
        (sum2, 0, 3 * narrow), (sum2, 3 * narrow, narrow), (summ, 0, wide),
        (sum3, 0, 3 * wide), (sum3, 3 * wide, wide),
    )
    for (source, offset, width), flat, room in zip(views, flats, rooms, strict=True):
        steps = width // LANES
        for j in range(steps):
            piece = source[:, offset + j * LANES : offset + (j + 1) * LANES]
            room[pl.ds(j, source.shape[0], stride=steps), :] = piece.astype(F32)
        flat[...] = room[...].astype(BF16)


def on_device(
    tokens, cotangent, shifts, norm2_gain, qkv2, proj2, merge_gain, merge_weight, norm3_gain,
    qkv3, proj3,
):
    rows, cols, narrow = tokens.shape
    wide = qkv3.shape[0]
    rows3, cols3 = rows // 2, cols // 2
    pitch, pitch3 = pitch_of(cols), pitch_of(cols3)
    base, base3 = rows * pitch, rows3 * pitch3
    win2, win3 = window_tokens(rows, cols), window_tokens(rows3, cols3)
    n2, n3 = len(win2[0]), len(win3[0])
    quad = quad_tokens(rows, cols)
    nat = grid_tokens(rows, cols, pitch)
    grid3 = grid_tokens(rows3, cols3, pitch3)
    as_grid = lambda h, w: h * pitch + w
    as_quad = lambda h, w: quad_index(h, w, rows, cols)
    as_win = lambda h, w: win_index(h, w, cols)
    as_win3 = lambda h, w: win_index(h, w, cols3)
    fixed = lambda t, inner: np.where(t[2], inner(t[0], t[1]), -1).astype(np.int32).reshape(-1, 1)

    idx_q = fixed(quad, as_grid)
    idx_n = fixed(nat, as_quad)
    idx_b = piece_index(rows, cols, as_win, False)
    idx_e = piece_index(rows3, cols3, as_win3, False)
    idx_g = piece_index(rows, cols, as_quad, True)
    gain2, gainm, gain3 = (g.reshape(1, -1) for g in (norm2_gain, merge_gain, norm3_gain))
    nr, nc = lax.axis_size("rows"), lax.axis_size("cols")
    chips = nc // 2
    quads, gains = len(quad[0]), 5 * narrow + wide
    inputs = dict(
        tok=tokens, cot=cotangent, shifts=shifts, win2=coded(win2), win3=coded(win3),
        rwin2=coded(win2).reshape(-1, SLOT), rwin3=coded(win3).reshape(-1, SLOT),
        quad=coded(quad), nat=coded(nat), grid3=coded(grid3), idx_b=idx_b, idx_e=idx_e,
        idx_g=idx_g, idx_n=idx_n, idx_q=idx_q, gain2=gain2, gainm=gainm, gain3=gain3, qkv2=qkv2, proj2=proj2,
        weight=merge_weight, qkv3=qkv3, proj3=proj3,
    )
    m3, mm, m2 = wide // (nr * nc), 4 * narrow // (nr * nc), narrow // (nr * nc)
    outs = dict(
        out=(cotangent.shape, BF16),
        dtok=(tokens.shape, BF16),
        gains=((1, gains), F32),
        sum3=((m3, 4 * wide), BF16),
        summ=((mm, wide), BF16),
        sum2=((m2, 4 * narrow), BF16),
    )
    row2, col2, cor = MARGIN * pitch, rows * PM, MARGIN * PM
    row3, col3 = MARGIN * pitch3, rows3 * PM
    scratch = dict(
        toks=((base, narrow), BF16), tside=((col2, narrow), BF16),
        cots=((base3, wide), BF16), cside=((col3, wide), BF16),
        rolled=((n2, narrow), BF16), packed=((n2, 3 * narrow), BF16), mixed=((n2, narrow), BF16),
        joined=((base3, 4 * narrow), BF16), mnorm=((base3, 4 * narrow), BF16),
        merged=((base3, wide), BF16), normed3=((base3, wide), BF16), nside=((col3, wide), BF16),
        packed3=((n3, 3 * wide), BF16), mixed3=((n3, wide), BF16),
        dpacked3=((n3, 3 * wide), BF16), both=((n3, 2 * wide), BF16),
        dsec=((quads, narrow), BF16), dpacked=((n2, 3 * narrow), BF16),
        row1=((row2, narrow), BF16), col1=((col2, narrow), BF16),
        row2=((row3, 2 * wide), BF16), col2=((col3, 2 * wide), BF16),
        row3=((row2, narrow), BF16), col3=((col2, narrow), BF16),
        row4=((row2, narrow), BF16), col4=((col2, narrow), BF16),
    )
    ints = dict(lc2=(n2, 1), lr2=(n2 // SLOT, SLOT), lc3=(n3, 1), lr3=(n3 // SLOT, SLOT))
    scratch |= {name: (shape, jnp.int32) for name, shape in ints.items()}
    copies = 7 * 3
    for n, (big, width) in enumerate(
        ((1, narrow), (0, wide), (1, narrow), (0, wide), (0, 2 * wide), (1, narrow), (1, narrow))
    ):
        for i, size in enumerate((row2, col2, cor) if big else (row3, col3, cor)):
            scratch[f"h{n}_{i}"] = ((size, width), BF16)
    for name, shape in (("g3", (m3, 4 * wide)), ("gm", (mm, wide)), ("g2", (m2, 4 * narrow))):
        scratch[name] = ((2, chips, nr) + shape, BF16)
        for i, lead in enumerate(
            ((chips, nr), (chips, nr), (max(chips - 1, 1), nr), (nr,), (max(nr - 1, 1),))
        ):
            scratch[f"{name}_{i}"] = (lead + shape, BF16)
        copies += 2 * chips + nr - 2
    for i, lead in enumerate(((), (), (), (max(chips - 1, 1),), (), (max(nr - 1, 1),))):
        scratch[f"gg_{i}"] = (lead + (1, gains), F32)
    copies += chips + nr - 1
    spaces = [pltpu.VMEM(s, d) for s, d in scratch.values()]
    spaces += [pltpu.SemaphoreType.DMA((copies,)), pltpu.SemaphoreType.DMA((copies,))]
    results = pl.pallas_call(
        functools.partial(
            whole_kernel, list(inputs), list(outs), list(scratch) + ["send", "recv"]
        ),
        out_shape=[jax.ShapeDtypeStruct(s, d) for s, d in outs.values()],
        in_specs=[
            pl.BlockSpec(memory_space=pltpu.SMEM if name == "shifts" else pltpu.VMEM)
            for name in inputs
        ],
        out_specs=[pl.BlockSpec(memory_space=pltpu.VMEM)] * len(outs),
        scratch_shapes=spaces,
        compiler_params=pltpu.CompilerParams(
            collective_id=0, has_side_effects=True, vmem_limit_bytes=60 * 2**20
        ),
        name="block",
    )(*inputs.values())
    flats = [
        (m * width // LANES, LANES)
        for m, width in (
            (m2, 3 * narrow), (m2, narrow), (mm, wide), (m3, 3 * wide), (m3, wide)
        )
    ]
    final = pl.pallas_call(
        finish_kernel,
        out_shape=[
            jax.ShapeDtypeStruct(cotangent.shape, BF16),
            jax.ShapeDtypeStruct(tokens.shape, BF16),
            jax.ShapeDtypeStruct((gains // LANES, LANES), F32),
        ]
        + [jax.ShapeDtypeStruct(shape, BF16) for shape in flats],
        scratch_shapes=[pltpu.VMEM(shape, F32) for shape in flats],
        name="finish",
    )(*results)
    return tuple(final[:2]) + tuple(x.reshape(-1) for x in final[2:])


def solution(mesh):
    tile = P(("groups", "rows"), "cols", None)
    spread = P(("groups", "rows", "cols"))
    return jax.shard_map(
        on_device,
        mesh=mesh,
        in_specs=(tile, tile) + (P(),) * 9,
        out_specs=(tile, tile, P("groups")) + (spread,) * 5,
        check_vma=False,
    )
```

```python
import functools

import jax
import jax.numpy as jnp
import numpy as np
from jax import lax
from jax.experimental import pallas as pl
from jax.experimental.pallas import tpu as pltpu
from jax.sharding import PartitionSpec as P

HEAD = 32
WIN = 7
MARGIN = WIN - 1
SLOT = 64
PM = 16
LANES = 128
EPSILON = 1e-05
MASKED = -100.0
F32 = jnp.float32
BF16 = jnp.bfloat16


def pitch_of(count):
    return -(-count // 16) * 16


def window_tokens(rows, cols):
    h, w, ok = [], [], []
    for wr in range(rows // WIN):
        for wc in range(cols // WIN):
            for t in range(SLOT):
                good = t < WIN * WIN
                h.append(wr * WIN + t // WIN if good else 0)
                w.append(wc * WIN + t % WIN if good else 0)
                ok.append(good)
    return np.array(h, np.int32), np.array(w, np.int32), np.array(ok)


def grid_tokens(rows, cols, pitch):
    h = np.repeat(np.arange(rows, dtype=np.int32), pitch)
    w = np.tile(np.arange(pitch, dtype=np.int32), rows)
    ok = w < cols
    return h, np.where(ok, w, 0).astype(np.int32), ok


def quad_tokens(rows, cols):
    a, b, ok = grid_tokens(rows // 2, cols // 2, pitch_of(cols // 2))
    h = np.concatenate([2 * a + (k & 1) for k in range(4)])
    w = np.concatenate([2 * b + (k >> 1) for k in range(4)])
    return h, w, np.tile(ok, 4)


def by_window(x):
    return (x * 9363) >> 16


def win_index(h, w, cols):
    hq, wq = by_window(h), by_window(w)
    return (hq * (cols // WIN) + wq) * SLOT + (h - hq * WIN) * WIN + w - wq * WIN


def quad_index(h, w, rows, cols):
    pitch = pitch_of(cols // 2)
    return ((h & 1) + 2 * (w & 1)) * ((rows // 2) * pitch) + (h >> 1) * pitch + (w >> 1)


def coded(tokens):
    h, w, ok = tokens
    return np.where(ok, h * 4096 + w, -1).astype(np.int32).reshape(-1, 1)


def decoded(code):
    return code >> 12, code & 4095, code >= 0


def ahead_index(code, shift_rows, shift_cols, rows, cols, inner, base):
    h, w, ok = decoded(code)
    pitch = pitch_of(cols)
    h2, w2 = h + shift_rows, w + shift_cols
    local = inner(jnp.minimum(h2, rows - 1), jnp.minimum(w2, cols - 1))
    below = base + (h2 - rows) * pitch + w2
    side = base + MARGIN * pitch + h2 * PM + (w2 - cols)
    return jnp.where(ok, jnp.where(w2 >= cols, side, jnp.where(h2 >= rows, below, local)), -1)


def behind_index(code, shift_rows, shift_cols, rows, cols, base):
    h, w, ok = decoded(code)
    pitch = pitch_of(cols)
    h2, w2 = h - shift_rows, w - shift_cols
    local = win_index(jnp.maximum(h2, 0), jnp.maximum(w2, 0), cols)
    above = base + (h2 + MARGIN) * pitch + w2
    row = jnp.where(h2 >= 0, h2, rows + h2 + MARGIN)
    side = base + MARGIN * pitch + row * PM + (w2 + MARGIN)
    return jnp.where(ok, jnp.where(w2 < 0, side, jnp.where(h2 < 0, above, local)), -1)


def piece_index(rows, cols, inner, first):
    top = 0 if first else rows - MARGIN
    left = 0 if first else cols - MARGIN
    parts = []
    for count, wide, pitch, h0, w0 in (
        (MARGIN, cols, pitch_of(cols), top, 0),
        (rows, MARGIN, PM, 0, left),
    ):
        h, w, ok = grid_tokens(count, wide, pitch)
        parts.append(np.where(ok, inner(h + h0, w + w0), -1))
    return np.concatenate(parts).astype(np.int32).reshape(-1, 1)


def window_labels(code, rows, cols, axis_row, axis_col, shift_rows, shift_cols):
    h, w, ok = decoded(code)
    height = rows * lax.axis_size("rows")
    breadth = cols * lax.axis_size("cols")
    gh = axis_row * rows + h
    gw = axis_col * cols + w
    lh = jnp.where(gh < height - WIN, 0, jnp.where(gh < height - shift_rows, 1, 2))
    lw = jnp.where(gw < breadth - WIN, 0, jnp.where(gw < breadth - shift_cols, 1, 2))
    return jnp.where(ok, lh * 3 + lw, -1)


def dot(a, b):
    return jnp.dot(a, b, preferred_element_type=F32)


def dot_nt(a, b):
    return lax.dot_general(a, b, (((1,), (1,)), ((), ())), preferred_element_type=F32)


def dot_tn(a, b):
    return lax.dot_general(a, b, (((0,), (0,)), ((), ())), preferred_element_type=F32)


def one_hot(idx, count):
    lane = lax.broadcasted_iota(jnp.int32, (idx.shape[0], count), 1)
    return jnp.where(idx == lane, 1.0, 0.0).astype(BF16)


def picked(hot, source):
    return dot(hot, source).astype(BF16)


def select(idx, source):
    return picked(one_hot(idx, source.shape[0]), source)


def norm_parts(x):
    centred = x - jnp.mean(x, axis=-1, keepdims=True)
    inverse = lax.rsqrt(jnp.mean(centred * centred, axis=-1, keepdims=True) + EPSILON)
    return centred * inverse, inverse


def norm_back(hat, inverse, gain, dy):
    grad_gain = jnp.sum(dy * hat, axis=0, keepdims=True)
    t = dy * gain
    dx = inverse * (
        t
        - jnp.mean(t, axis=-1, keepdims=True)
        - hat * jnp.mean(t * hat, axis=-1, keepdims=True)
    )
    return dx.astype(BF16), grad_gain


PACK = LANES // HEAD


def head_masks():
    lane = lax.broadcasted_iota(jnp.int32, (1, LANES), 1) // HEAD
    return [jnp.where(lane == h, 1.0, 0.0).astype(BF16) for h in range(PACK)]


def stack_heads(x, masks):
    return jnp.concatenate([x * m for m in masks], axis=0)


def pick_heads(o):
    lane = lax.broadcasted_iota(jnp.int32, (SLOT, LANES), 1) // HEAD
    out = o[:SLOT]
    for h in range(1, PACK):
        out = jnp.where(lane == h, o[h * SLOT : (h + 1) * SLOT], out)
    return out


def window_bias(lc_ref, lr_ref, w):
    lc = lc_ref[w * SLOT : (w + 1) * SLOT, :]
    lr = lr_ref[w : w + 1, :]
    bias = jnp.where((lc == lr) | (lc < 0), 0.0, MASKED)
    bias = jnp.where(lr < 0, -1e30, bias)
    return jnp.concatenate([bias] * PACK, axis=0)


def soft(qs, k, bias):
    raised = jnp.exp(dot_nt(qs, k) * HEAD ** (-0.5) + bias)
    return raised * (1.0 / jnp.sum(raised, axis=-1, keepdims=True))


def unit_back(qs, k, v, weights, wb, dm, masks):
    dms = stack_heads(dm, masks)
    dw = dot_nt(dms, v).astype(BF16).astype(F32)
    ds = weights * (dw - jnp.sum(dw * weights, axis=-1, keepdims=True))
    ds = (ds * HEAD ** (-0.5)).astype(BF16)
    dq = pick_heads(dot(ds, k))
    dk = dot_tn(ds, qs)
    dv = dot_tn(wb, dms)
    return dq.astype(BF16), dk.astype(BF16), dv.astype(BF16)


def fill_tile(scratch, tile, pitch):
    count, wide, _ = tile.shape
    for r in range(count):
        scratch[r * pitch : r * pitch + wide, :] = tile[r]


class Bag:
    pass


MESH = pl.DeviceIdType.MESH


class Links:
    def __init__(self, send, recv):
        self.send, self.recv, self.used = send, recv, 0
        self.group = lax.axis_index("groups")
        self.row, self.col = lax.axis_index("rows"), lax.axis_index("cols")
        self.nr, self.nc = lax.axis_size("rows"), lax.axis_size("cols")
        self.core, self.chip = lax.rem(self.col, 2), self.col // 2
        self.chips = self.nc // 2

    def device(self, dr, dc):
        row = lax.rem(self.row + dr + self.nr, self.nr)
        col = lax.rem(self.col + dc + self.nc, self.nc)
        return (self.group, row, col)

    def partner(self):
        return (self.group, self.row, self.chip * 2 + 1 - self.core)

    def barrier(self):
        offsets = {(d, 0) for d in range(1, self.nr)} | {(0, d) for d in range(1, self.nc)}
        offsets |= {(1, 1), (self.nr - 1, self.nc - 1)}
        sem = pltpu.get_barrier_semaphore()
        for dr, dc in sorted(offsets):
            pl.semaphore_signal(sem, inc=1, device_id=self.device(dr, dc), device_id_type=MESH)
        pl.semaphore_wait(sem, len(offsets))

    def start(self, source, target, device):
        copy = pltpu.make_async_remote_copy(
            src_ref=source,
            dst_ref=target,
            send_sem=self.send.at[self.used],
            recv_sem=self.recv.at[self.used],
            device_id=device,
            device_id_type=MESH,
        )
        self.used += 1
        copy.start()
        return copy

    def exchange(self, row, col, corner, halo, by):
        return [
            self.start(row, halo[0], self.device(by, 0)),
            self.start(col, halo[1], self.device(0, by)),
            self.start(corner, halo[2], self.device(by, by)),
        ]


def wait_all(copies):
    for copy in copies:
        copy.wait()


class Reduction:
    def __init__(self, links, kind, parts, bufs):
        self.links, self.kind, self.parts = links, kind, parts
        self.got1, self.half, self.got2, self.part, self.got3 = bufs


    def start_first(self, d):
        k = self.links
        x = lax.rem(k.chip + d, k.chips)
        return k.start(self.parts.at[1 - k.core, x], self.got1.at[x], k.partner())

    def first_away(self):
        self.away = [self.start_first(d) for d in range(1, self.links.chips)]

    def first_own(self):
        self.own = self.start_first(0)

    def both_cores(self, x, r):
        return self.parts[self.links.core, x, r].astype(F32) + self.got1[x, r].astype(F32)

    def second(self):
        k = self.links
        wait_all(self.away)
        self.copies = []
        for d in range(1, k.chips):
            x = lax.rem(k.chip + d, k.chips)
            for r in range(k.nr):
                self.half[x, r] = self.both_cores(x, r).astype(self.kind)
            self.copies.append(k.start(self.half.at[x], self.got2.at[d - 1], k.device(0, 2 * d)))

    def third(self):
        k = self.links
        wait_all([self.own] + self.copies)
        for r in range(k.nr):
            total = self.both_cores(k.chip, r)
            for d in range(1, k.chips):
                total = total + self.got2[d - 1, r].astype(F32)
            self.part[r] = total.astype(self.kind)
        self.copies = [
            k.start(self.part.at[lax.rem(k.row + d, k.nr)], self.got3.at[d - 1], k.device(d, 0))
            for d in range(1, k.nr)
        ]

    def finish(self):
        k = self.links
        wait_all(self.copies)
        total = self.part[k.row].astype(F32)
        for d in range(1, k.nr):
            total = total + self.got3[d - 1].astype(F32)
        return total


class GainSum:
    def __init__(self, links, bufs):
        self.links = links
        self.own, self.got1, self.half, self.got2, self.part, self.got3 = bufs

    def first(self):
        self.copies = [self.links.start(self.own, self.got1, self.links.partner())]

    def second(self):
        k = self.links
        wait_all(self.copies)
        self.half[...] = self.own[...] + self.got1[...]
        self.copies = [
            k.start(self.half, self.got2.at[d - 1], k.device(0, 2 * d)) for d in range(1, k.chips)
        ]

    def third(self):
        k = self.links
        wait_all(self.copies)
        total = self.half[...]
        for d in range(1, k.chips):
            total = total + self.got2[d - 1]
        self.part[...] = total
        self.copies = [k.start(self.part, self.got3.at[d - 1], k.device(d, 0)) for d in range(1, k.nr)]

    def finish(self):
        wait_all(self.copies)
        total = self.part[...]
        for d in range(1, self.links.nr):
            total = total + self.got3[d - 1]
        return total


def store_parts(parts, value, offset):
    _, chips, nr, depth, _ = parts.shape
    width = value.shape[1]
    for r in range(nr):
        for x in range(chips):
            for core in range(2):
                i = (r * chips + x) * 2 + core
                piece = value[i * depth : (i + 1) * depth]
                parts[core, x, r, :, offset : offset + width] = piece.astype(BF16)


def fill_side(scratch, tile):
    scratch[...] = jnp.zeros_like(scratch)
    for r in range(tile.shape[0]):
        scratch[r * PM : r * PM + MARGIN, :] = tile[r, :MARGIN, :]


def put_pieces(idx, source, row_ref, col_ref):
    got = select(idx[...], source)
    row_ref[...] = got[: row_ref.shape[0]]
    col_ref[...] = got[row_ref.shape[0] :]


def lanes_of(width, g):
    return [slice(t * width + g * LANES, t * width + (g + 1) * LANES) for t in range(3)]


def joined_ext(first, halo):
    return jnp.concatenate([first] + [h[...] for h in halo], axis=0)


def whole_kernel(in_names, out_names, scratch_names, *refs):
    b = Bag()
    for name, ref in zip(in_names + out_names + scratch_names, refs, strict=True):
        setattr(b, name, ref)
    links = Links(b.send, b.recv)
    rows, cols, narrow = b.tok.shape
    rows3, cols3, wide = b.cot.shape
    pitch, pitch3 = pitch_of(cols), pitch_of(cols3)
    red3 = Reduction(links, BF16, b.g3, [getattr(b, f"g3_{i}") for i in range(5)])
    redm = Reduction(links, BF16, b.gm, [getattr(b, f"gm_{i}") for i in range(5)])
    red2 = Reduction(links, BF16, b.g2, [getattr(b, f"g2_{i}") for i in range(5)])
    redg = GainSum(links, [getattr(b, f"gg_{i}") for i in range(6)])
    halos = [[getattr(b, f"h{n}_{i}") for i in range(3)] for n in range(7)]
    margin2 = slice(0, MARGIN * PM)
    masks = head_masks()
    s0, s1, s2, s3 = (b.shifts[i] for i in range(4))
    quads, quad_pitch = b.quad.shape[0], pitch_of(cols // 2)
    n2, n3 = b.win2.shape[0], b.win3.shape[0]
    base, base3 = rows * pitch, rows3 * pitch3
    as_grid = lambda h, w: h * pitch + w
    as_grid3 = lambda h, w: h * pitch3 + w
    as_quad = lambda h, w: quad_index(h, w, rows, cols)
    extra = MARGIN * pitch + (rows + MARGIN) * PM
    extra3 = MARGIN * pitch3 + (rows3 + MARGIN) * PM

    b.toks[...] = jnp.zeros_like(b.toks)
    fill_tile(b.toks, b.tok, pitch)
    fill_side(b.tside, b.tok)
    b.cots[...] = jnp.zeros_like(b.cots)
    fill_tile(b.cots, b.cot, pitch3)
    fill_side(b.cside, b.cot)
    links.barrier()
    flying = links.exchange(
        b.toks.at[0 : MARGIN * pitch], b.tside, b.tside.at[margin2], halos[0], -1
    )
    flying_c = links.exchange(
        b.cots.at[0 : MARGIN * pitch3], b.cside, b.cside.at[margin2], halos[1], -1
    )

    place2 = (rows, cols, links.row, links.col, s0, s1)
    place3 = (rows3, cols3, links.row, links.col, s2, s3)
    b.lc2[...] = window_labels(b.win2[...], *place2)
    b.lr2[...] = window_labels(b.rwin2[...], *place2)
    b.lc3[...] = window_labels(b.win3[...], *place3)
    b.lr3[...] = window_labels(b.rwin3[...], *place3)
    quad = select(b.idx_q[...], b.toks[...])
    idx = ahead_index(b.win2[...], s0, s1, rows, cols, as_grid, base)
    hot = one_hot(idx, base + extra)
    wait_all(flying)
    hat, _ = norm_parts(picked(hot, joined_ext(b.toks[...], halos[0])).astype(F32))
    b.rolled[...] = (hat * b.gain2[...]).astype(BF16)
    b.packed[...] = dot(b.rolled[...], b.qkv2[...]).astype(BF16)
    for w in range(b.lr2.shape[0]):
        bias = window_bias(b.lc2, b.lr2, w)
        at = slice(w * SLOT, (w + 1) * SLOT)
        for g in range(narrow // LANES):
            lanes = lanes_of(narrow, g)
            qs = stack_heads(b.packed[at, lanes[0]], masks)
            wb = soft(qs, b.packed[at, lanes[1]], bias).astype(BF16)
            b.mixed[at, lanes[0]] = pick_heads(dot(wb, b.packed[at, lanes[2]])).astype(BF16)
    win = dot(b.mixed[...], b.proj2[...]).astype(BF16)
    put_pieces(b.idx_b, win, b.row1, b.col1)
    last2 = slice((rows - MARGIN) * PM, rows * PM)
    flying = links.exchange(b.row1, b.col1, b.col1.at[last2], halos[2], 1)

    hot = one_hot(behind_index(b.quad[...], s0, s1, rows, cols, n2), n2 + extra)
    wait_all(flying)
    restored = picked(hot, joined_ext(win, halos[2]))
    section = (quad.astype(F32) + restored.astype(F32)).astype(BF16)
    t3 = rows3 * pitch3
    joined = jnp.concatenate([section[k * t3 : (k + 1) * t3] for k in range(4)], axis=1)
    b.joined[...] = joined
    hat, _ = norm_parts(joined.astype(F32))
    b.mnorm[...] = (hat * b.gainm[...]).astype(BF16)
    b.merged[...] = dot(b.mnorm[...], b.weight[...]).astype(BF16)
    hat, _ = norm_parts(b.merged[...].astype(F32))
    normed3 = (hat * b.gain3[...]).astype(BF16)
    b.normed3[...] = normed3
    for r in range(rows3):
        b.nside[r * PM : (r + 1) * PM, :] = normed3[r * pitch3 : r * pitch3 + PM]
    flying = links.exchange(
        b.normed3.at[0 : MARGIN * pitch3], b.nside, b.nside.at[margin2], halos[3], -1
    )

    wait_all(flying_c)
    idx = ahead_index(b.win3[...], s2, s3, rows3, cols3, as_grid3, base3)
    hot = one_hot(idx, base3 + extra3)
    dproj = picked(hot, joined_ext(b.cots[...], halos[1]))
    dmixed = dot_nt(dproj, b.proj3[...]).astype(BF16)
    wait_all(flying)
    rolled3 = picked(hot, joined_ext(b.normed3[...], halos[3]))
    b.packed3[...] = dot(rolled3, b.qkv3[...]).astype(BF16)
    for w in range(b.lr3.shape[0]):
        bias = window_bias(b.lc3, b.lr3, w)
        at = slice(w * SLOT, (w + 1) * SLOT)
        for g in range(wide // LANES):
            lanes = lanes_of(wide, g)
            qs = stack_heads(b.packed3[at, lanes[0]], masks)
            k, v = b.packed3[at, lanes[1]], b.packed3[at, lanes[2]]
            weights = soft(qs, k, bias)
            wb = weights.astype(BF16)
            b.mixed3[at, lanes[0]] = pick_heads(dot(wb, v)).astype(BF16)
            back = unit_back(qs, k, v, weights, wb, dmixed[at, lanes[0]], masks)
            for t in range(3):
                b.dpacked3[at, lanes[t]] = back[t]
    b.both[:, :wide] = dot(b.mixed3[...], b.proj3[...]).astype(BF16)
    b.both[:, wide:] = dot_nt(b.dpacked3[...], b.qkv3[...]).astype(BF16)
    put_pieces(b.idx_e, b.both[...], b.row2, b.col2)
    last3 = slice((rows3 - MARGIN) * PM, rows3 * PM)
    flying = links.exchange(b.row2, b.col2, b.col2.at[last3], halos[4], 1)
    store_parts(b.g3, dot_tn(rolled3, b.dpacked3[...]), 0)
    store_parts(b.g3, dot_tn(b.mixed3[...], dproj), 3 * wide)
    red3.first_away()

    hot = one_hot(behind_index(b.grid3[...], s2, s3, rows3, cols3, n3), n3 + extra3)
    wait_all(flying)
    back = picked(hot, joined_ext(b.both[...], halos[4]))
    mine = b.merged[...].astype(F32)
    total = (mine + back[:, :wide].astype(F32)).astype(BF16)
    for r in range(rows3):
        b.out[r] = total[r * pitch3 : r * pitch3 + cols3]
    hat, inv = norm_parts(mine)
    dmerged, grad3 = norm_back(hat, inv, b.gain3[...], back[:, wide:].astype(F32))
    dmerged = b.cots[...] + dmerged
    hat, inv = norm_parts(b.joined[...].astype(F32))
    djn = dot_nt(dmerged, b.weight[...]).astype(BF16).astype(F32)
    djoined, gradm = norm_back(hat, inv, b.gainm[...], djn)
    b.gg_0[:, narrow : 5 * narrow] = gradm
    b.gg_0[:, 5 * narrow :] = grad3
    b.dsec[...] = jnp.concatenate(
        [djoined[:, k * narrow : (k + 1) * narrow] for k in range(4)], axis=0
    )
    put_pieces(b.idx_g, b.dsec[...], b.row3, b.col3)
    flying = links.exchange(b.row3, b.col3, b.col3.at[margin2], halos[5], -1)
    red3.first_own()
    store_parts(b.gm, dot_tn(b.mnorm[...], dmerged), 0)
    redm.first_away()
    redm.first_own()
    red3.second()

    idx = ahead_index(b.win2[...], s0, s1, rows, cols, as_quad, quads)
    hot = one_hot(idx, quads + extra)
    wait_all(flying)
    dproj = picked(hot, joined_ext(b.dsec[...], halos[5]))
    dmixed = dot_nt(dproj, b.proj2[...]).astype(BF16)
    for w in range(b.lr2.shape[0]):
        bias = window_bias(b.lc2, b.lr2, w)
        at = slice(w * SLOT, (w + 1) * SLOT)
        for g in range(narrow // LANES):
            lanes = lanes_of(narrow, g)
            qs = stack_heads(b.packed[at, lanes[0]], masks)
            k, v = b.packed[at, lanes[1]], b.packed[at, lanes[2]]
            weights = soft(qs, k, bias)
            back = unit_back(
                qs, k, v, weights, weights.astype(BF16), dmixed[at, lanes[0]], masks
            )
            for t in range(3):
                b.dpacked[at, lanes[t]] = back[t]
    drolled = dot_nt(b.dpacked[...], b.qkv2[...]).astype(BF16)
    put_pieces(b.idx_b, drolled, b.row4, b.col4)
    flying = links.exchange(b.row4, b.col4, b.col4.at[last2], halos[6], 1)
    store_parts(b.g2, dot_tn(b.rolled[...], b.dpacked[...]), 0)
    store_parts(b.g2, dot_tn(b.mixed[...], dproj), 3 * narrow)
    red2.first_away()
    red2.first_own()
    red3.third()
    redm.second()

    hot = one_hot(behind_index(b.nat[...], s0, s1, rows, cols, n2), n2 + extra)
    wait_all(flying)
    dnormed = picked(hot, joined_ext(drolled, halos[6])).astype(F32)
    hat, inv = norm_parts(b.toks[...].astype(F32))
    dtok, grad2 = norm_back(hat, inv, b.gain2[...], dnormed)
    b.gg_0[:, :narrow] = grad2
    redg.first()
    red2.second()
    total = select(b.idx_n[...], b.dsec[...]) + dtok
    for r in range(rows):
        b.dtok[r] = total[r * pitch : r * pitch + cols]
    redg.second()
    redm.third()
    red2.third()
    redg.third()
    b.sum3[...] = red3.finish().astype(BF16)
    b.summ[...] = redm.finish().astype(BF16)
    b.sum2[...] = red2.finish().astype(BF16)
    b.gains[...] = redg.finish()


def finish_kernel(out, dtok, gains, sum3, summ, sum2, o_out, o_dtok, o_gains, *rest):
    o_out[...] = out[...]
    o_dtok[...] = dtok[...]
    for j in range(o_gains.shape[0]):
        o_gains[j : j + 1, :] = gains[:, j * LANES : (j + 1) * LANES]
    flats, rooms = rest[: len(rest) // 2], rest[len(rest) // 2 :]
    wide, narrow = sum3.shape[1] // 4, sum2.shape[1] // 4
    views = (
        (sum2, 0, 3 * narrow), (sum2, 3 * narrow, narrow), (summ, 0, wide),
        (sum3, 0, 3 * wide), (sum3, 3 * wide, wide),
    )
    for (source, offset, width), flat, room in zip(views, flats, rooms, strict=True):
        steps = width // LANES
        for j in range(steps):
            piece = source[:, offset + j * LANES : offset + (j + 1) * LANES]
            room[pl.ds(j, source.shape[0], stride=steps), :] = piece.astype(F32)
        flat[...] = room[...].astype(BF16)


def on_device(
    tokens, cotangent, shifts, norm2_gain, qkv2, proj2, merge_gain, merge_weight, norm3_gain,
    qkv3, proj3,
):
    rows, cols, narrow = tokens.shape
    wide = qkv3.shape[0]
    rows3, cols3 = rows // 2, cols // 2
    pitch, pitch3 = pitch_of(cols), pitch_of(cols3)
    base, base3 = rows * pitch, rows3 * pitch3
    win2, win3 = window_tokens(rows, cols), window_tokens(rows3, cols3)
    n2, n3 = len(win2[0]), len(win3[0])
    quad = quad_tokens(rows, cols)
    nat = grid_tokens(rows, cols, pitch)
    grid3 = grid_tokens(rows3, cols3, pitch3)
    as_grid = lambda h, w: h * pitch + w
    as_quad = lambda h, w: quad_index(h, w, rows, cols)
    as_win = lambda h, w: win_index(h, w, cols)
    as_win3 = lambda h, w: win_index(h, w, cols3)
    fixed = lambda t, inner: np.where(t[2], inner(t[0], t[1]), -1).astype(np.int32).reshape(-1, 1)

    idx_q = fixed(quad, as_grid)
    idx_n = fixed(nat, as_quad)
    idx_b = piece_index(rows, cols, as_win, False)
    idx_e = piece_index(rows3, cols3, as_win3, False)
    idx_g = piece_index(rows, cols, as_quad, True)
    gain2, gainm, gain3 = (g.reshape(1, -1) for g in (norm2_gain, merge_gain, norm3_gain))
    nr, nc = lax.axis_size("rows"), lax.axis_size("cols")
    chips = nc // 2
    quads, gains = len(quad[0]), 5 * narrow + wide
    inputs = dict(
        tok=tokens, cot=cotangent, shifts=shifts, win2=coded(win2), win3=coded(win3),
        rwin2=coded(win2).reshape(-1, SLOT), rwin3=coded(win3).reshape(-1, SLOT),
        quad=coded(quad), nat=coded(nat), grid3=coded(grid3), idx_b=idx_b, idx_e=idx_e,
        idx_g=idx_g, idx_n=idx_n, idx_q=idx_q, gain2=gain2, gainm=gainm, gain3=gain3, qkv2=qkv2, proj2=proj2,
        weight=merge_weight, qkv3=qkv3, proj3=proj3,
    )
    m3, mm, m2 = wide // (nr * nc), 4 * narrow // (nr * nc), narrow // (nr * nc)
    outs = dict(
        out=(cotangent.shape, BF16),
        dtok=(tokens.shape, BF16),
        gains=((1, gains), F32),
        sum3=((m3, 4 * wide), BF16),
        summ=((mm, wide), BF16),
        sum2=((m2, 4 * narrow), BF16),
    )
    row2, col2, cor = MARGIN * pitch, rows * PM, MARGIN * PM
    row3, col3 = MARGIN * pitch3, rows3 * PM
    scratch = dict(
        toks=((base, narrow), BF16), tside=((col2, narrow), BF16),
        cots=((base3, wide), BF16), cside=((col3, wide), BF16),
        rolled=((n2, narrow), BF16), packed=((n2, 3 * narrow), BF16), mixed=((n2, narrow), BF16),
        joined=((base3, 4 * narrow), BF16), mnorm=((base3, 4 * narrow), BF16),
        merged=((base3, wide), BF16), normed3=((base3, wide), BF16), nside=((col3, wide), BF16),
        packed3=((n3, 3 * wide), BF16), mixed3=((n3, wide), BF16),
        dpacked3=((n3, 3 * wide), BF16), both=((n3, 2 * wide), BF16),
        dsec=((quads, narrow), BF16), dpacked=((n2, 3 * narrow), BF16),
        row1=((row2, narrow), BF16), col1=((col2, narrow), BF16),
        row2=((row3, 2 * wide), BF16), col2=((col3, 2 * wide), BF16),
        row3=((row2, narrow), BF16), col3=((col2, narrow), BF16),
        row4=((row2, narrow), BF16), col4=((col2, narrow), BF16),
    )
    ints = dict(lc2=(n2, 1), lr2=(n2 // SLOT, SLOT), lc3=(n3, 1), lr3=(n3 // SLOT, SLOT))
    scratch |= {name: (shape, jnp.int32) for name, shape in ints.items()}
    copies = 7 * 3
    for n, (big, width) in enumerate(
        ((1, narrow), (0, wide), (1, narrow), (0, wide), (0, 2 * wide), (1, narrow), (1, narrow))
    ):
        for i, size in enumerate((row2, col2, cor) if big else (row3, col3, cor)):
            scratch[f"h{n}_{i}"] = ((size, width), BF16)
    for name, shape in (("g3", (m3, 4 * wide)), ("gm", (mm, wide)), ("g2", (m2, 4 * narrow))):
        scratch[name] = ((2, chips, nr) + shape, BF16)
        for i, lead in enumerate(
            ((chips, nr), (chips, nr), (max(chips - 1, 1), nr), (nr,), (max(nr - 1, 1),))
        ):
            scratch[f"{name}_{i}"] = (lead + shape, BF16)
        copies += 2 * chips + nr - 2
    for i, lead in enumerate(((), (), (), (max(chips - 1, 1),), (), (max(nr - 1, 1),))):
        scratch[f"gg_{i}"] = (lead + (1, gains), F32)
    copies += chips + nr - 1
    spaces = [pltpu.VMEM(s, d) for s, d in scratch.values()]
    spaces += [pltpu.SemaphoreType.DMA((copies,)), pltpu.SemaphoreType.DMA((copies,))]
    results = pl.pallas_call(
        functools.partial(
            whole_kernel, list(inputs), list(outs), list(scratch) + ["send", "recv"]
        ),
        out_shape=[jax.ShapeDtypeStruct(s, d) for s, d in outs.values()],
        in_specs=[
            pl.BlockSpec(memory_space=pltpu.SMEM if name == "shifts" else pltpu.VMEM)
            for name in inputs
        ],
        out_specs=[pl.BlockSpec(memory_space=pltpu.VMEM)] * len(outs),
        scratch_shapes=spaces,
        compiler_params=pltpu.CompilerParams(
            collective_id=0, has_side_effects=True, vmem_limit_bytes=60 * 2**20
        ),
        name="block",
    )(*inputs.values())
    flats = [
        (m * width // LANES, LANES)
        for m, width in (
            (m2, 3 * narrow), (m2, narrow), (mm, wide), (m3, 3 * wide), (m3, wide)
        )
    ]
    final = pl.pallas_call(
        finish_kernel,
        out_shape=[
            jax.ShapeDtypeStruct(cotangent.shape, BF16),
            jax.ShapeDtypeStruct(tokens.shape, BF16),
            jax.ShapeDtypeStruct((gains // LANES, LANES), F32),
        ]
        + [jax.ShapeDtypeStruct(shape, BF16) for shape in flats],
        scratch_shapes=[pltpu.VMEM(shape, F32) for shape in flats],
        name="finish",
    )(*results)
    return tuple(final[:2]) + tuple(x.reshape(-1) for x in final[2:])


def solution(mesh):
    tile = P(("groups", "rows"), "cols", None)
    spread = P(("groups", "rows", "cols"))
    return jax.shard_map(
        on_device,
        mesh=mesh,
        in_specs=(tile, tile) + (P(),) * 9,
        out_specs=(tile, tile, P("groups")) + (spread,) * 5,
        check_vma=False,
    )
```
